256 devices in a mesh: dp: 8 (over z), ctx: 32 (over y, x, core).
Axes of the slice: x: 4, y: 4, z: 8, core: 2. Of those that a mesh axis runs over, the one named last changes fastest.
Arguments:
- queries: bfloat16 [65536, 256], P(('dp', 'ctx')), parts along dimension 0, may hold values from -64 to 64
- key_rows: bfloat16 [65536, 128], P(('dp', 'ctx')), parts along dimension 0, may hold values from -8 to 8
- value_rows: bfloat16 [65536, 128], P(('dp', 'ctx')), parts along dimension 0, may hold values from -6 to 6
- grad_output: bfloat16 [65536, 256], P(('dp', 'ctx')), parts along dimension 0, may hold values from -6 to 6
- doc_lengths: int32 [128], P('dp'), parts along dimension 0, may hold values from 1 to 2048, 8192 in all
- block_order: int32 [512], P('dp'), parts along dimension 0, may hold values from 0 to 63, each once
Outputs:
- attention: bfloat16 [65536, 256], P(('dp', 'ctx')), parts along dimension 0
- grad_queries: bfloat16 [65536, 256], P(('dp', 'ctx')), parts along dimension 0
- grad_keys: bfloat16 [65536, 128], P(('dp', 'ctx')), parts along dimension 0
- grad_values: bfloat16 [65536, 128], P(('dp', 'ctx')), parts along dimension 0
The draws below stay inside these ranges and needn't reach their ends.
There are 8 independent parts, one for each index of `dp`. The reference program is written for one: setup_inputs(seed, part) draws one part's arguments, and reference() takes and returns one part's arrays. A program takes and returns all parts, laid end to end along the dimension named above; each array names one. Nothing has to cross between parts.
Inputs may be any that keep to these rules, and one draw needn't show every extreme that they name: `doc_lengths`: 16 lengths summing to 8192, the longest exactly 2048. `block_order`: each of the 64 block numbers once.
All inputs are finite; a program needn't handle non-finite values.
Results may differ from the reference program's by a relative error of at most 0.035.
Values may be sent and summed in bfloat16 or wider, within the bound.
No kernel may reach another device: no remote copies, remote signals or barrier semaphores. Data moves between devices by JAX's collectives and lax.ppermute only.
A program may use at most 64 MiB of HBM per device.

```python
import math
import jax
import jax.numpy as jnp
import numpy as np
from jax import lax

HD = 128
QHEADS = 2
TOK_DEV = 256
BLK = 128
NDOC = 16
SEQ = 8192
NBLK = 64
DOC_MAX = 2048
N_CTX = 32


def joint_rows(key):
    key_base = jax.random.fold_in(key, 7101)
    key_query = jax.random.fold_in(key, 7102)
    keys = jax.random.truncated_normal(key_base, -6.0, 6.0, (SEQ, HD), jnp.float32)
    query = jax.random.truncated_normal(key_query, -6.0, 6.0, (SEQ, QHEADS * HD), jnp.float32)
    return (query, keys)


def draw_queries(key, part):
    return joint_rows(key)[0].astype(jnp.bfloat16)


def draw_key_rows(key, part):
    return joint_rows(key)[1].astype(jnp.bfloat16)


def level_of(stream_key, dims, cuts, smallest, top_value):
    loudness, own = 1.0, jax.random.fold_in(stream_key, 6)
    for dim, shards_of in cuts:
        draws = jnp.exp(jax.random.uniform(jax.random.fold_in(own, dim), (shards_of,), jnp.float32, smallest / len(cuts), top_value / len(cuts)))
        loudness = loudness * jnp.repeat(draws, dims[dim] // shards_of).reshape([-1 if axis == dim else 1 for axis in range(len(dims))])
    return loudness


def profile(count, total, bound, slope):
    loads = [(1 << 20) // math.isqrt(rank ** slope) + 1 for rank in range(2, count + 1)]
    rest, given = total - bound - (count - 1), [1] * (count - 1)
    while rest > 0:
        free = [i for i in range(count - 1) if given[i] < bound]
        mass, remaining = sum([loads[i] for i in free]), rest
        for i in free:
            extra = min(bound - given[i], max(1, remaining * loads[i] // mass), rest)
            given[i] = given[i] + extra
            rest = rest - extra
    return np.array([bound] + given)


def uneven_parts(rng, number_of, total, bound, lean):
    if number_of == 2:
        one = jax.random.randint(rng, (), max(1, total - bound), min(bound, total - 1) + 1)
        return jnp.stack([one, total - one])
    lengths = jnp.asarray(profile(number_of, total, bound, lean), jnp.int32)
    couples = (number_of - 1) // 2
    source_of, taker = lengths[1:1 + 2 * couples:2], lengths[2:2 + 2 * couples:2]
    margin = jnp.minimum(source_of - 1, bound - taker)
    shifted = jax.random.randint(jax.random.fold_in(rng, 1), (couples,), 0, 1 << 20) % (margin + 1)
    lengths = lengths.at[1:1 + 2 * couples:2].set(source_of - shifted).at[2:2 + 2 * couples:2].set(taker + shifted)
    return lengths[jax.random.permutation(jax.random.fold_in(rng, 2), number_of)]


def bell_draw(key, shape, scale, most, cuts=(), held_as=jnp.bfloat16):
    factor_of = level_of(key, shape, cuts, -0.22, 0.18) if cuts else 1.0
    array = jax.random.normal(key, shape, jnp.float32) * scale * factor_of
    return jnp.minimum(jnp.maximum(array, -most), most).astype(held_as)


def setup_inputs(seed: int = 0, part: int = 0) -> dict:
    key_of = jax.random.split(jax.random.key(seed), 7)
    own_keys = jax.random.split(jax.random.fold_in(key_of[6], part), 7)
    return {
        "queries": draw_queries(jax.random.fold_in(jax.random.fold_in(key_of[6], part), 71), part),
        "key_rows": draw_key_rows(jax.random.fold_in(jax.random.fold_in(key_of[6], part), 71), part),
        "value_rows": bell_draw(own_keys[2], (SEQ, HD), 1.0, 6.0, ((0, 32),)),
        "grad_output": bell_draw(own_keys[3], (SEQ, QHEADS * HD), 1.0, 6.0, ((0, 32),)),
        "doc_lengths": uneven_parts(own_keys[4], NDOC, SEQ, DOC_MAX, 2).astype(jnp.int32),
        "block_order": jax.random.permutation(own_keys[5], NBLK).astype(jnp.int32),
    }


NEG = -1.0e30


def locate(block_order, count):
    rows = jnp.arange(count, dtype=jnp.int32)
    which = rows // BLK
    table = jnp.arange(block_order.shape[0], dtype=jnp.int32)
    picked = jnp.sum(jnp.where(which[:, None] == table[None, :], block_order[None, :], 0), axis=1)
    return (picked * BLK + rows % BLK).astype(jnp.int32)


def reference(queries, key_rows, value_rows, grad_output, doc_lengths, block_order):
    scale = HD ** -0.5
    ends = jnp.cumsum(doc_lengths)
    places = locate(block_order, SEQ)
    docs = jnp.sum((ends[None, :] <= places[:, None]).astype(jnp.int32), axis=1)
    query_all = queries.astype(jnp.float32).reshape(SEQ, QHEADS, HD)
    grad_all = grad_output.astype(jnp.float32).reshape(SEQ, QHEADS, HD)
    keys32 = key_rows.astype(jnp.float32)
    values32 = value_rows.astype(jnp.float32)
    high = lax.Precision.HIGHEST

    def one_block(carry, index):
        grad_k, grad_v = carry
        start = (index * TOK_DEV).astype(jnp.int32)
        qry = lax.dynamic_slice_in_dim(query_all, start, TOK_DEV, 0)
        gout = lax.dynamic_slice_in_dim(grad_all, start, TOK_DEV, 0)
        qpos = lax.dynamic_slice_in_dim(places, start, TOK_DEV, 0)
        qdoc = lax.dynamic_slice_in_dim(docs, start, TOK_DEV, 0)
        allowed = (qdoc[:, None] == docs[None, :]) & (places[None, :] <= qpos[:, None])
        raw = jnp.einsum("qhd,kd->hqk", qry, keys32, precision=high) * scale
        top = jnp.max(jnp.where(allowed, raw, NEG), axis=2)
        total = jnp.sum(jnp.where(allowed, jnp.exp(raw - top[..., None]), 0.0), axis=2)
        logsum = top + jnp.log(total)
        prob = jnp.where(allowed, jnp.exp(raw - logsum[..., None]), 0.0)
        weights = lax.optimization_barrier(prob.astype(jnp.bfloat16)).astype(jnp.float32)
        output = jnp.einsum("hqk,kd->qhd", weights, values32, precision=high).astype(jnp.bfloat16)
        delta = jnp.sum(gout * output.astype(jnp.float32), axis=2).T
        dprob = jnp.einsum("qhd,kd->hqk", gout, values32, precision=high)
        dscore = prob * (dprob - delta[..., None]) * scale
        dscore = lax.optimization_barrier(dscore.astype(jnp.bfloat16)).astype(jnp.float32)
        grad_q = jnp.einsum("hqk,kd->qhd", dscore, keys32, precision=high).astype(jnp.bfloat16)
        grad_k = grad_k + jnp.einsum("hqk,qhd->kd", dscore, qry, precision=high)
        grad_v = grad_v + jnp.einsum("hqk,qhd->kd", weights, gout, precision=high)
        return (grad_k, grad_v), (output, grad_q)

    zeros = jnp.zeros((SEQ, HD), jnp.float32)
    (grad_k, grad_v), (outputs, grad_qs) = lax.scan(one_block, (zeros, zeros), jnp.arange(N_CTX, dtype=jnp.int32))
    attention = outputs.reshape(SEQ, QHEADS * HD)
    grad_queries = grad_qs.reshape(SEQ, QHEADS * HD)
    return attention, grad_queries, grad_k.astype(jnp.bfloat16), grad_v.astype(jnp.bfloat16)
```

```python
import functools

import jax
import jax.numpy as jnp
from jax import lax
from jax.experimental import pallas as pl
from jax.experimental.pallas import tpu as pltpu
from jax.sharding import PartitionSpec as P

BLK = 128
HD = 128
NBLK = 64
NDOC = 16
SIDE = 4
CHUNK = 4
WINDOW = 20
NEG = -1e30
SCALE = HD**-0.5
LOG2E = 1.4426950408889634
SCALE2 = SCALE * LOG2E

NT = (((1,), (1,)), ((), ()))
NN = (((1,), (0,)), ((), ()))
TN = (((0,), (0,)), ((), ()))


def device_of(y, x, core):
    return (y % SIDE) * 2 * SIDE + (x % SIDE) * 2 + core


def along(axis_of_core):
    groups = []
    for core in range(2):
        for fixed in range(SIDE):
            if axis_of_core[core] == "y":
                groups.append([device_of(i, fixed, core) for i in range(SIDE)])
            else:
                groups.append([device_of(fixed, i, core) for i in range(SIDE)])
    return groups


FIRST = along("yx")
SECOND = along("xy")
SWAP = [(i, i ^ 1) for i in range(2 * SIDE * SIDE)]


def mm(a, b, dims):
    return lax.dot_general(a, b, dims, preferred_element_type=jnp.float32)


def attend(order, lengths, q_ref, g_ref, own_ref, oth_ref, o_ref, dq_ref, dkv_own, dkv_oth, kv, s_ref, acc, table):
    me = lax.axis_index("ctx")
    core = me % 2
    half = NBLK // 2

    def place(s, _):
        dev = s // 2
        y, x, c = dev // (2 * SIDE), (dev // 2) % SIDE, dev % 2
        slot = jnp.where(c == 0, x * SIDE + y, y * SIDE + x)
        plane = jnp.where(c == core, 0, 1)
        table[order[s]] = plane * half + slot * 2 + s % 2
        return 0

    lax.fori_loop(0, NBLK, place, 0)
    acc[...] = jnp.zeros_like(acc)
    kv[pl.ds(0, half * BLK), :] = own_ref[...]
    kv[pl.ds(half * BLK, half * BLK), :] = oth_ref[...]

    lane = lax.broadcasted_iota(jnp.int32, (1, 2 * BLK), 1) % BLK
    sub = lax.broadcasted_iota(jnp.int32, (BLK, 2 * BLK), 0)

    for i in range(2):
        blk = order[2 * me + i]
        qpos = blk * BLK + lane
        end, low = jnp.int32(0), jnp.int32(0)
        qstart = jnp.zeros((1, 2 * BLK), jnp.int32)
        for d in range(NDOC):
            end = end + lengths[d]
            qstart = jnp.where(qpos >= end, end, qstart)
            low = jnp.where(blk * BLK >= end, end, low)
        count = blk - low // BLK + 1
        trips = (count + CHUNK - 1) // CHUNK

        rows = pl.ds(i * BLK, BLK)
        qs = jnp.concatenate([q_ref[rows, :HD], q_ref[rows, HD:]], axis=0)
        gs = jnp.concatenate([g_ref[rows, :HD], g_ref[rows, HD:]], axis=0)

        def row_of(t, j):
            p = jnp.maximum(blk - (t * CHUNK + j), 0)
            return pl.multiple_of(table[p] * BLK, BLK)

        def load(t, cols):
            return jnp.concatenate([kv[pl.ds(row_of(t, j), BLK), cols] for j in range(CHUNK)], axis=0)

        keys, vals = slice(0, HD), slice(HD, 2 * HD)

        def scores(t, top):
            s = mm(load(t, keys), qs, NT)
            for j in range(CHUNK):
                kpos = (blk - (t * CHUNK + j)) * BLK + sub
                ok = (kpos >= qstart) & (kpos <= qpos)
                part = jnp.where(ok, s[j * BLK : (j + 1) * BLK], NEG)
                s_ref[pl.ds(pl.multiple_of((t * CHUNK + j) * BLK, BLK), BLK), :] = part
                top = jnp.maximum(top, jnp.max(part, axis=0, keepdims=True))
            return top

        top = lax.fori_loop(0, trips, scores, jnp.full((1, 2 * BLK), NEG, jnp.float32))

        def outputs(t, carry):
            total, out = carry
            at = pl.ds(pl.multiple_of(t * CHUNK * BLK, CHUNK * BLK), CHUNK * BLK)
            p = jnp.exp2((s_ref[at, :] - top) * SCALE2)
            s_ref[at, :] = p
            total = total + jnp.sum(p, axis=0, keepdims=True)
            out = out + mm(load(t, vals), p.astype(jnp.bfloat16), TN)
            return total, out

        total, out = lax.fori_loop(
            0, trips, outputs, (jnp.zeros((1, 2 * BLK), jnp.float32), jnp.zeros((HD, 2 * BLK), jnp.float32))
        )
        inv = 1.0 / total
        att = (out * inv).T.astype(jnp.bfloat16)
        o_ref[rows, :HD] = att[:BLK]
        o_ref[rows, HD:] = att[BLK:]
        prod = gs.astype(jnp.float32) * att.astype(jnp.float32)
        delta = jnp.sum(prod.T, axis=0, keepdims=True)

        def grads(t, dq):
            at = pl.ds(pl.multiple_of(t * CHUNK * BLK, CHUNK * BLK), CHUNK * BLK)
            p = s_ref[at, :] * inv
            dp = mm(load(t, vals), gs, NT)
            ds = (p * (dp - delta) * SCALE).astype(jnp.bfloat16)
            dv = mm(p.astype(jnp.bfloat16), gs, NN)
            dk = mm(ds, qs, NN)
            dq = dq + mm(load(t, keys), ds, TN)
            for j in range(CHUNK):
                to = pl.ds(row_of(t, j), BLK)
                acc[to, keys] += dk[j * BLK : (j + 1) * BLK]
                acc[to, vals] += dv[j * BLK : (j + 1) * BLK]
            return dq

        dq = lax.fori_loop(0, trips, grads, jnp.zeros((HD, 2 * BLK), jnp.float32)).T.astype(jnp.bfloat16)
        dq_ref[rows, :HD] = dq[:BLK]
        dq_ref[rows, HD:] = dq[BLK:]

    dkv_own[...] = acc[pl.ds(0, half * BLK), :].astype(jnp.bfloat16)
    dkv_oth[...] = acc[pl.ds(half * BLK, half * BLK), :].astype(jnp.bfloat16)


def attention_kernel(order, lengths, queries, grad, own, oth):
    tokens = queries.shape[0]
    rows = own.shape[0]
    vmem = pl.BlockSpec(memory_space=pltpu.VMEM)
    bf16 = jnp.bfloat16
    return pl.pallas_call(
        attend,
        out_shape=(
            jax.ShapeDtypeStruct((tokens, 2 * HD), bf16),
            jax.ShapeDtypeStruct((tokens, 2 * HD), bf16),
            jax.ShapeDtypeStruct((rows, 2 * HD), bf16),
            jax.ShapeDtypeStruct((rows, 2 * HD), bf16),
        ),
        in_specs=[pl.BlockSpec(memory_space=pltpu.SMEM)] * 2 + [vmem] * 4,
        out_specs=(vmem,) * 4,
        scratch_shapes=[
            pltpu.VMEM((2 * rows, 2 * HD), bf16),
            pltpu.VMEM((WINDOW * BLK, 2 * BLK), jnp.float32),
            pltpu.VMEM((2 * rows, 2 * HD), jnp.float32),
            pltpu.SMEM((NBLK,), jnp.int32),
        ],
        compiler_params=pltpu.CompilerParams(vmem_limit_bytes=50 * 1024 * 1024),
        name="attend",
    )(order, lengths, queries, grad, own, oth)


def per_device(queries, key_rows, value_rows, grad_output, doc_lengths, block_order):
    tokens = queries.shape[0]
    kv = jnp.concatenate([key_rows, value_rows], axis=1)
    line = lax.all_gather(kv, "ctx", axis=0, tiled=True, axis_index_groups=FIRST)
    spread = jnp.broadcast_to(line[None], (SIDE,) + line.shape)
    own = lax.all_to_all(spread, "ctx", 0, 0, tiled=True, axis_index_groups=SECOND)
    own = own.reshape(SIDE * SIDE * tokens, 2 * HD)
    oth = lax.ppermute(own, "ctx", SWAP)
    attention, grad_queries, dkv_own, dkv_oth = attention_kernel(
        block_order, doc_lengths, queries, grad_output, own, oth
    )
    back = lax.ppermute(dkv_oth, "ctx", SWAP)
    f32 = jnp.float32
    part = (dkv_own.astype(f32) + back.astype(f32)).astype(jnp.bfloat16)
    part = part.reshape(SIDE, SIDE * tokens, 2 * HD)
    part = lax.all_to_all(part, "ctx", 0, 0, tiled=True, axis_index_groups=SECOND)
    part = jnp.sum(part.astype(f32), axis=0).astype(jnp.bfloat16).reshape(SIDE, tokens, 2 * HD)
    part = lax.all_to_all(part, "ctx", 0, 0, tiled=True, axis_index_groups=FIRST)
    part = jnp.sum(part.astype(f32), axis=0).astype(jnp.bfloat16)
    return attention, grad_queries, part[:, :HD], part[:, HD:]


def solution(mesh):
    rows = P(("dp", "ctx"), None)
    return jax.shard_map(
        per_device,
        mesh=mesh,
        in_specs=(rows, rows, rows, rows, P("dp"), P("dp")),
        out_specs=(rows, rows, rows, rows),
        check_vma=False,
    )
```

```python
import jax
import jax.numpy as jnp
from jax import lax
from jax.experimental import pallas as pl
from jax.experimental.pallas import tpu as pltpu
from jax.sharding import PartitionSpec as P

BLK = 128
HD = 128
NBLK = 64
NDOC = 16
SIDE = 4
HALF = NBLK // 2
CHUNK = 4
REACH = 17
LIST = 24
ROWS_AT = 4 * LIST
COUNT_AT = 8 * LIST
META = 256
NEG = -1e30
SCALE = HD**-0.5
SCALE2 = SCALE * 1.4426950408889634
LANES = 2 * BLK

NT = (((1,), (1,)), ((), ()))
NN = (((1,), (0,)), ((), ()))
TN = (((0,), (0,)), ((), ()))
KEYS, VALS = slice(0, HD), slice(HD, 2 * HD)


def device_of(y, x, core):
    return (y % SIDE) * 2 * SIDE + (x % SIDE) * 2 + core


def along(axis_of_core):
    groups = []
    for core in range(2):
        for fixed in range(SIDE):
            if axis_of_core[core] == "y":
                groups.append([device_of(i, fixed, core) for i in range(SIDE)])
            else:
                groups.append([device_of(fixed, i, core) for i in range(SIDE)])
    return groups


FIRST = along("yx")
SECOND = along("xy")
SWAP = [(i, i ^ 1) for i in range(2 * SIDE * SIDE)]


def mm(a, b, dims):
    return lax.dot_general(a, b, dims, preferred_element_type=jnp.float32)


def stacked(ref, i):
    rows = pl.ds(i * BLK, BLK)
    return jnp.concatenate([ref[rows, :HD], ref[rows, HD:]], axis=0)


def unstack(ref, i, value):
    rows = pl.ds(i * BLK, BLK)
    ref[rows, :HD] = value[:BLK]
    ref[rows, HD:] = value[BLK:]


def place(meta, base, n):
    return pl.multiple_of(meta[ROWS_AT + base + n] * BLK, BLK)


def load(kv, meta, base, t, cols):
    return jnp.concatenate(
        [kv[pl.ds(place(meta, base, t * CHUNK + j), BLK), cols] for j in range(CHUNK)], axis=0
    )


def masked(s, meta, vec, i, base, t, sub):
    qstart, qpos = vec[2 * i : 2 * i + 1, :], vec[2 * i + 1 : 2 * i + 2, :]
    parts = []
    for j in range(CHUNK):
        first = meta[base + t * CHUNK + j] * BLK
        ok = (sub >= qstart - first) & (sub <= qpos - first)
        parts.append(jnp.where(ok, s[j * BLK : (j + 1) * BLK], NEG))
    return parts


def trips_of(meta, i, plane):
    return (meta[COUNT_AT + 2 * i + plane] + CHUNK - 1) // CHUNK


def iota_sub():
    return lax.broadcasted_iota(jnp.int32, (BLK, LANES), 0)


def chunk_at(t):
    return pl.ds(pl.multiple_of(t * CHUNK * BLK, CHUNK * BLK), CHUNK * BLK)


def tops(parts):
    best = jnp.maximum(jnp.maximum(parts[0], parts[1]), jnp.maximum(parts[2], parts[3]))
    return jnp.max(best, axis=0, keepdims=True)


def first_pass(order, lengths, q_ref, own_hbm, meta, vec, stat, part, kv, table, sem):
    copy = pltpu.make_async_copy(own_hbm, kv, sem)
    copy.start()
    me = lax.axis_index("ctx")
    core = me % 2

    def find(s, _):
        dev = s // 2
        y, x, c = dev // (2 * SIDE), (dev // 2) % SIDE, dev % 2
        slot = jnp.where(c == 0, x * SIDE + y, y * SIDE + x) * 2 + s % 2
        table[order[s]] = jnp.where(c == core, slot, slot + HALF)
        return 0

    lax.fori_loop(0, NBLK, find, 0, unroll=8)
    lane = lax.broadcasted_iota(jnp.int32, (1, LANES), 1) & (BLK - 1)
    for i in range(2):
        blk = order[2 * me + i]
        qpos = blk * BLK + lane
        end, low = jnp.int32(0), jnp.int32(0)
        qstart = jnp.zeros((1, LANES), jnp.int32)
        for d in range(NDOC):
            end = end + lengths[d]
            qstart = jnp.where(qpos >= end, end, qstart)
            low = jnp.where(blk * BLK >= end, end, low)
        vec[2 * i : 2 * i + 1, :] = qstart
        vec[2 * i + 1 : 2 * i + 2, :] = qpos
        low = low // BLK
        mine, others = jnp.int32(2 * i * LIST), jnp.int32((2 * i + 1) * LIST)
        for j in range(REACH):
            p = blk - j
            slot = table[jnp.maximum(p, 0)]
            away = slot >= HALF
            at = jnp.where(away, others, mine)
            meta[at] = p
            meta[ROWS_AT + at] = slot & (HALF - 1)
            step = jnp.where(p >= low, 1, 0)
            others = others + jnp.where(away, step, 0)
            mine = mine + jnp.where(away, 0, step)
        meta[COUNT_AT + 2 * i] = mine - 2 * i * LIST
        meta[COUNT_AT + 2 * i + 1] = others - (2 * i + 1) * LIST
        for j in range(CHUNK):
            for at in (mine, others):
                meta[at + j] = -1024
                meta[ROWS_AT + at + j] = 0
    copy.wait()
    sub = iota_sub()
    for i in range(2):
        qs = stacked(q_ref, i)
        base = 2 * i * LIST

        def step(t, carry):
            top, total, out = carry
            s = mm(load(kv, meta, base, t, KEYS), qs, NT)
            parts = masked(s, meta, vec, i, base, t, sub)
            new = jnp.maximum(top, tops(parts))
            shrink = jnp.exp2((top - new) * SCALE2)
            p = jnp.exp2((jnp.concatenate(parts, axis=0) - new) * SCALE2)
            total = total * shrink + jnp.sum(p, axis=0, keepdims=True)
            out = out * shrink + mm(load(kv, meta, base, t, VALS), p.astype(jnp.bfloat16), TN)
            return new, total, out

        top, total, out = lax.fori_loop(
            0,
            trips_of(meta, i, 0),
            step,
            (
                jnp.full((1, LANES), NEG, jnp.float32),
                jnp.zeros((1, LANES), jnp.float32),
                jnp.zeros((HD, LANES), jnp.float32),
            ),
        )
        stat[2 * i : 2 * i + 1, :] = top
        stat[2 * i + 1 : 2 * i + 2, :] = total
        part[i] = out


def add_to(ref, meta, base, t, dk, dv):
    for j in range(CHUNK):
        to = pl.ds(place(meta, base, t * CHUNK + j), BLK)
        rows = slice(j * BLK, (j + 1) * BLK)
        ref[to, KEYS] = (ref[to, KEYS].astype(jnp.float32) + dk[rows]).astype(jnp.bfloat16)
        ref[to, VALS] = (ref[to, VALS].astype(jnp.float32) + dv[rows]).astype(jnp.bfloat16)


def second_pass(meta, vec, stat, q_ref, g_ref, part, oth_hbm, o_ref, lse, dq_ref, dkv, kv, s_ref, p_ref, sem):
    copy = pltpu.make_async_copy(oth_hbm, kv, sem)
    copy.start()
    dkv[...] = jnp.zeros_like(dkv)
    sub = iota_sub()
    copy.wait()
    for i in range(2):
        qs, gs = stacked(q_ref, i), stacked(g_ref, i)
        base = (2 * i + 1) * LIST
        trips = trips_of(meta, i, 1)
        old_top, old_total = stat[2 * i : 2 * i + 1, :], stat[2 * i + 1 : 2 * i + 2, :]

        def scores(t, top):
            s = mm(load(kv, meta, base, t, KEYS), qs, NT)
            parts = masked(s, meta, vec, i, base, t, sub)
            s_ref[chunk_at(t), :] = jnp.concatenate(parts, axis=0)
            return jnp.maximum(top, tops(parts))

        top = lax.fori_loop(0, trips, scores, old_top)
        shrink = jnp.exp2((old_top - top) * SCALE2)

        def outputs(t, carry):
            total, out = carry
            p = jnp.exp2((s_ref[chunk_at(t), :] - top) * SCALE2)
            total = total + jnp.sum(p, axis=0, keepdims=True)
            p = p.astype(jnp.bfloat16)
            p_ref[chunk_at(t), :] = p
            return total, out + mm(load(kv, meta, base, t, VALS), p, TN)

        total, out = lax.fori_loop(0, trips, outputs, (old_total * shrink, part[i] * shrink))
        inv = 1.0 / total
        att = (out * inv).T.astype(jnp.bfloat16)
        unstack(o_ref, i, att)
        delta = jnp.sum((gs.astype(jnp.float32) * att.astype(jnp.float32)).T, axis=0, keepdims=True)
        lse[2 * i : 2 * i + 1, :] = top * SCALE2 + jnp.log2(total)
        lse[2 * i + 1 : 2 * i + 2, :] = delta
        scaled = inv * SCALE

        def grads(t, dq):
            p = p_ref[chunk_at(t), :].astype(jnp.float32)
            dp = mm(load(kv, meta, base, t, VALS), gs, NT)
            ds = ((p * scaled) * (dp - delta)).astype(jnp.bfloat16)
            dv = mm((p * inv).astype(jnp.bfloat16), gs, NN)
            dk = mm(ds, qs, NN)
            add_to(dkv, meta, base, t, dk, dv)
            return dq + mm(load(kv, meta, base, t, KEYS), ds, TN)

        dq_ref[i] = lax.fori_loop(0, trips, grads, jnp.zeros((HD, LANES), jnp.float32))


def third_pass(meta, vec, lse, q_ref, g_ref, dq_in, own_hbm, dq_ref, dkv, kv, sem):
    copy = pltpu.make_async_copy(own_hbm, kv, sem)
    copy.start()
    dkv[...] = jnp.zeros_like(dkv)
    sub = iota_sub()
    copy.wait()
    for i in range(2):
        qs, gs = stacked(q_ref, i), stacked(g_ref, i)
        base = 2 * i * LIST
        logsum, delta = lse[2 * i : 2 * i + 1, :], lse[2 * i + 1 : 2 * i + 2, :]

        def grads(t, dq):
            keys = load(kv, meta, base, t, KEYS)
            parts = masked(mm(keys, qs, NT), meta, vec, i, base, t, sub)
            p = jnp.exp2(jnp.concatenate(parts, axis=0) * SCALE2 - logsum)
            dp = mm(load(kv, meta, base, t, VALS), gs, NT)
            ds = ((p * SCALE) * (dp - delta)).astype(jnp.bfloat16)
            dv = mm(p.astype(jnp.bfloat16), gs, NN)
            dk = mm(ds, qs, NN)
            add_to(dkv, meta, base, t, dk, dv)
            return dq + mm(keys, ds, TN)

        dq = lax.fori_loop(0, trips_of(meta, i, 0), grads, dq_in[i])
        unstack(dq_ref, i, dq.T.astype(jnp.bfloat16))


SMEM = pl.BlockSpec(memory_space=pltpu.SMEM)
VMEM = pl.BlockSpec(memory_space=pltpu.VMEM)
ANY = pl.BlockSpec(memory_space=pl.ANY)


def shape(*dims, dtype=jnp.bfloat16):
    return jax.ShapeDtypeStruct(dims, dtype)


def kernel(body, name, ins, outs, out_specs, scratch, flops, size):
    return pl.pallas_call(
        body,
        out_shape=outs,
        in_specs=ins,
        out_specs=out_specs,
        scratch_shapes=scratch,
        compiler_params=pltpu.CompilerParams(vmem_limit_bytes=48 * 1024 * 1024),
        cost_estimate=pl.CostEstimate(flops=flops, bytes_accessed=size, transcendentals=0),
        name=name,
    )


def per_device(queries, key_rows, value_rows, grad_output, doc_lengths, block_order):
    tokens = queries.shape[0]
    f32, i32, bf16 = jnp.float32, jnp.int32, jnp.bfloat16
    plane = HALF * BLK
    buffer = pltpu.VMEM((plane, 2 * HD), bf16)
    sem = pltpu.SemaphoreType.DMA
    kv = jnp.concatenate([key_rows, value_rows], axis=1)
    line = lax.all_gather(kv, "ctx", axis=0, tiled=True, axis_index_groups=FIRST)
    spread = jnp.broadcast_to(line[None], (SIDE,) + line.shape)
    own = lax.all_to_all(spread, "ctx", 0, 0, tiled=True, axis_index_groups=SECOND)
    own = own.reshape(plane, 2 * HD)
    oth = lax.ppermute(own, "ctx", SWAP)
    wide = shape(2, HD, LANES, dtype=f32)
    small = shape(4, LANES, dtype=f32)
    meta, vec, stat, part = kernel(
        first_pass,
        "forward_own",
        [SMEM, SMEM, VMEM, ANY],
        (shape(META, dtype=i32), shape(4, LANES, dtype=i32), small, wide),
        (SMEM, VMEM, VMEM, VMEM),
        [buffer, pltpu.SMEM((NBLK,), i32), sem],
        2 * 10**9,
        4 * 10**6,
    )(block_order, doc_lengths, queries, own)
    attention, lse, dq, dkv_oth = kernel(
        second_pass,
        "other_plane",
        [SMEM, VMEM, VMEM, VMEM, VMEM, VMEM, ANY],
        (shape(tokens, 2 * HD), small, wide, shape(plane, 2 * HD)),
        (VMEM,) * 4,
        [buffer, pltpu.VMEM((LIST * BLK, LANES), f32), pltpu.VMEM((LIST * BLK, LANES), bf16), sem],
        4 * 10**9,
        6 * 10**6,
    )(meta, vec, stat, queries, grad_output, part, oth)
    back = lax.ppermute(dkv_oth, "ctx", SWAP)
    grad_queries, dkv_own = kernel(
        third_pass,
        "backward_own",
        [SMEM, VMEM, VMEM, VMEM, VMEM, VMEM, ANY],
        (shape(tokens, 2 * HD), shape(plane, 2 * HD)),
        (VMEM,) * 2,
        [buffer, sem],
        3 * 10**9,
        6 * 10**6,
    )(meta, vec, lse, queries, grad_output, dq, own)
    part = (dkv_own.astype(f32) + back.astype(f32)).astype(bf16)
    part = part.reshape(SIDE, SIDE * tokens, 2 * HD)
    part = lax.all_to_all(part, "ctx", 0, 0, tiled=True, axis_index_groups=SECOND)
    part = jnp.sum(part.astype(f32), axis=0).astype(bf16).reshape(SIDE, tokens, 2 * HD)
    part = lax.all_to_all(part, "ctx", 0, 0, tiled=True, axis_index_groups=FIRST)
    part = jnp.sum(part.astype(f32), axis=0).astype(bf16)
    return attention, grad_queries, part[:, :HD], part[:, HD:]


def solution(mesh):
    rows = P(("dp", "ctx"), None)
    return jax.shard_map(
        per_device,
        mesh=mesh,
        in_specs=(rows, rows, rows, rows, P("dp"), P("dp")),
        out_specs=(rows, rows, rows, rows),
        check_vma=False,
    )
```

```python
import jax
import jax.numpy as jnp
from jax import lax
from jax.experimental import pallas as pl
from jax.experimental.pallas import tpu as pltpu
from jax.sharding import PartitionSpec as P

BLK = 128
HD = 128
NBLK = 64
NDOC = 16
SIDE = 4
HALF = NBLK // 2
CHUNK = 4
REACH = 17
LIST = 24
ROWS_AT = 4 * LIST
COUNT_AT = 8 * LIST
META = 256
NEG = -1e30
SCALE = HD**-0.5
SCALE2 = SCALE * 1.4426950408889634
LANES = 2 * BLK

NT = (((1,), (1,)), ((), ()))
NN = (((1,), (0,)), ((), ()))
TN = (((0,), (0,)), ((), ()))
KEYS, VALS = slice(0, HD), slice(HD, 2 * HD)


def device_of(y, x, core):
    return (y % SIDE) * 2 * SIDE + (x % SIDE) * 2 + core


def along(axis_of_core):
    groups = []
    for core in range(2):
        for fixed in range(SIDE):
            if axis_of_core[core] == "y":
                groups.append([device_of(i, fixed, core) for i in range(SIDE)])
            else:
                groups.append([device_of(fixed, i, core) for i in range(SIDE)])
    return groups


FIRST = along("yx")
SECOND = along("xy")
SWAP = [(i, i ^ 1) for i in range(2 * SIDE * SIDE)]


def mm(a, b, dims):
    return lax.dot_general(a, b, dims, preferred_element_type=jnp.float32)


def stacked(ref, i):
    rows = pl.ds(i * BLK, BLK)
    return jnp.concatenate([ref[rows, :HD], ref[rows, HD:]], axis=0)


def unstack(ref, i, value):
    rows = pl.ds(i * BLK, BLK)
    ref[rows, :HD] = value[:BLK]
    ref[rows, HD:] = value[BLK:]


def place(meta, base, n):
    return pl.multiple_of(meta[ROWS_AT + base + n] * BLK, BLK)


def load(kv, meta, base, t, cols):
    return jnp.concatenate(
        [kv[pl.ds(place(meta, base, t * CHUNK + j), BLK), cols] for j in range(CHUNK)], axis=0
    )


def chunk_at(t):
    return pl.ds(pl.multiple_of(t * CHUNK * BLK, CHUNK * BLK), CHUNK * BLK)


def scores_of(keys, qs, meta, vec, i, base, t):
    s = mm(keys, qs, NT)
    sub = lax.broadcasted_iota(jnp.int32, (BLK, LANES), 0)
    qstart, qpos = vec[2 * i : 2 * i + 1, :], vec[2 * i + 1 : 2 * i + 2, :]
    parts = []
    for j in range(CHUNK):
        first = meta[base + t * CHUNK + j] * BLK
        ok = (sub >= qstart - first) & (sub <= qpos - first)
        parts.append(jnp.where(ok, s[j * BLK : (j + 1) * BLK], NEG))
    return jnp.concatenate(parts, axis=0)


def trips_of(meta, plane):
    most = jnp.maximum(meta[COUNT_AT + plane], meta[COUNT_AT + 2 + plane])
    return (most + CHUNK - 1) // CHUNK


def tops(s):
    return jnp.max(s, axis=0, keepdims=True)


def first_pass(order, lengths, q_ref, own_hbm, meta, vec, stat, part, kv, table, sem):
    copy = fetch_all(own_hbm, kv, sem)
    me = lax.axis_index("ctx")
    core = me & 1
    for s in range(NBLK):
        dev = s // 2
        y, x, c = dev // (2 * SIDE), (dev // 2) % SIDE, dev % 2
        slot = (y * SIDE + x if c else x * SIDE + y) * 2 + s % 2
        table[order[s]] = slot + (HALF * (1 - core) if c else HALF * core)
    lane = lax.broadcasted_iota(jnp.int32, (1, LANES), 1) & (BLK - 1)
    for i in range(2):
        blk = order[2 * me + i]
        qpos = blk * BLK + lane
        end, low = jnp.int32(0), jnp.int32(0)
        qstart = jnp.zeros((1, LANES), jnp.int32)
        for d in range(NDOC):
            end = end + lengths[d]
            qstart = jnp.where(qpos >= end, end, qstart)
            low = jnp.where(blk * BLK >= end, end, low)
        vec[2 * i : 2 * i + 1, :] = qstart
        vec[2 * i + 1 : 2 * i + 2, :] = qpos
        low = low >> 7
        for j in range(2 * LIST):
            meta[2 * i * LIST + j] = -1024
            meta[ROWS_AT + 2 * i * LIST + j] = 0
        mine, others = jnp.int32(2 * i * LIST), jnp.int32((2 * i + 1) * LIST)
        for j in range(REACH):
            p = blk - j
            slot = table[jnp.maximum(p, 0)]
            away = slot >= HALF
            at = jnp.where(away, others, mine)
            meta[at] = p
            meta[ROWS_AT + at] = slot & (HALF - 1)
            step = jnp.where(p >= low, 1, 0)
            others = others + jnp.where(away, step, 0)
            mine = mine + jnp.where(away, 0, step)
        meta[COUNT_AT + 2 * i] = mine - 2 * i * LIST
        meta[COUNT_AT + 2 * i + 1] = others - (2 * i + 1) * LIST
        meta[mine] = -1024
        meta[others] = -1024
    copy.wait()
    qs = [stacked(q_ref, i) for i in range(2)]

    def step(t, carry):
        after = []
        for i in range(2):
            top, total, out = carry[i]
            base = 2 * i * LIST
            s = scores_of(load(kv, meta, base, t, KEYS), qs[i], meta, vec, i, base, t)
            new = jnp.maximum(top, tops(s))
            shrink = jnp.exp2((top - new) * SCALE2)
            p = jnp.exp2((s - new) * SCALE2)
            total = total * shrink + jnp.sum(p, axis=0, keepdims=True)
            out = out * shrink + mm(load(kv, meta, base, t, VALS), p.astype(jnp.bfloat16), TN)
            after.append((new, total, out))
        return tuple(after)

    empty = (
        jnp.full((1, LANES), NEG, jnp.float32),
        jnp.zeros((1, LANES), jnp.float32),
        jnp.zeros((HD, LANES), jnp.float32),
    )
    for i, (top, total, out) in enumerate(lax.fori_loop(0, trips_of(meta, 0), step, (empty, empty))):
        stat[2 * i : 2 * i + 1, :] = top
        stat[2 * i + 1 : 2 * i + 2, :] = total
        part[i] = out


def fetch_all(hbm, kv, sem):
    copy = pltpu.make_async_copy(hbm, kv, sem)
    copy.start()
    return copy


def put(ref, meta, base, t, dk, dv):
    for j in range(CHUNK):
        to = pl.ds(place(meta, base, t * CHUNK + j), BLK)
        rows = slice(j * BLK, (j + 1) * BLK)
        ref[to, KEYS] = (ref[to, KEYS].astype(jnp.float32) + dk[rows]).astype(jnp.bfloat16)
        ref[to, VALS] = (ref[to, VALS].astype(jnp.float32) + dv[rows]).astype(jnp.bfloat16)


def second_pass(meta, vec, stat, q_ref, g_ref, part, oth_hbm, o_ref, lse, dq_ref, dkv, kv, s_ref, p_ref, sem):
    copy = fetch_all(oth_hbm, kv, sem)
    dkv[...] = jnp.zeros_like(dkv)
    copy.wait()
    both = range(2)
    qs, gs = [stacked(q_ref, i) for i in both], [stacked(g_ref, i) for i in both]
    base = [(2 * i + 1) * LIST for i in both]
    trips = trips_of(meta, 1)
    old_top = [stat[2 * i : 2 * i + 1, :] for i in both]

    def scores(t, tops_so_far):
        after = []
        for i in both:
            s = scores_of(load(kv, meta, base[i], t, KEYS), qs[i], meta, vec, i, base[i], t)
            s_ref[i, chunk_at(t), :] = s
            after.append(jnp.maximum(tops_so_far[i], tops(s)))
        return tuple(after)

    top = lax.fori_loop(0, trips, scores, tuple(old_top))

    def outputs(t, carry):
        after = []
        for i in both:
            total, out = carry[i]
            p = jnp.exp2((s_ref[i, chunk_at(t), :] - top[i]) * SCALE2)
            total = total + jnp.sum(p, axis=0, keepdims=True)
            p = p.astype(jnp.bfloat16)
            p_ref[i, chunk_at(t), :] = p
            after.append((total, out + mm(load(kv, meta, base[i], t, VALS), p, TN)))
        return tuple(after)

    start = []
    for i in both:
        shrink = jnp.exp2((old_top[i] - top[i]) * SCALE2)
        start.append((stat[2 * i + 1 : 2 * i + 2, :] * shrink, part[i] * shrink))
    done = lax.fori_loop(0, trips, outputs, tuple(start))
    scaled, delta, over = [], [], []
    for i in both:
        total, out = done[i]
        inv = 1.0 / total
        att = (out * inv).T.astype(jnp.bfloat16)
        unstack(o_ref, i, att)
        wide = gs[i].astype(jnp.float32)
        delta.append(jnp.sum((wide * att.astype(jnp.float32)).T, axis=0, keepdims=True))
        lse[2 * i : 2 * i + 1, :] = top[i] * SCALE2 + jnp.log2(total)
        lse[2 * i + 1 : 2 * i + 2, :] = delta[i]
        scaled.append(inv * SCALE)
        over.append((wide * jnp.broadcast_to(inv, (HD, LANES)).T).astype(jnp.bfloat16))

    def grads(t, dq):
        after = []
        for i in both:
            p = p_ref[i, chunk_at(t), :]
            dp = mm(load(kv, meta, base[i], t, VALS), gs[i], NT)
            ds = ((p.astype(jnp.float32) * scaled[i]) * (dp - delta[i])).astype(jnp.bfloat16)
            put(dkv, meta, base[i], t, mm(ds, qs[i], NN), mm(p, over[i], NN))
            after.append(dq[i] + mm(load(kv, meta, base[i], t, KEYS), ds, TN))
        return tuple(after)

    zero = jnp.zeros((HD, LANES), jnp.float32)
    dq_ref[0], dq_ref[1] = lax.fori_loop(0, trips, grads, (zero, zero))


def third_pass(meta, vec, lse, q_ref, g_ref, dq_in, own_hbm, dq_ref, dkv, kv, sem):
    copy = fetch_all(own_hbm, kv, sem)
    dkv[...] = jnp.zeros_like(dkv)
    copy.wait()
    both = range(2)
    qs, gs = [stacked(q_ref, i) for i in both], [stacked(g_ref, i) for i in both]

    def grads(t, dq):
        after = []
        for i in both:
            base = 2 * i * LIST
            keys = load(kv, meta, base, t, KEYS)
            s = scores_of(keys, qs[i], meta, vec, i, base, t)
            p = jnp.exp2(s * SCALE2 - lse[2 * i : 2 * i + 1, :])
            dp = mm(load(kv, meta, base, t, VALS), gs[i], NT)
            ds = ((p * SCALE) * (dp - lse[2 * i + 1 : 2 * i + 2, :])).astype(jnp.bfloat16)
            put(dkv, meta, base, t, mm(ds, qs[i], NN), mm(p.astype(jnp.bfloat16), gs[i], NN))
            after.append(dq[i] + mm(keys, ds, TN))
        return tuple(after)

    for i, dq in enumerate(lax.fori_loop(0, trips_of(meta, 0), grads, (dq_in[0], dq_in[1]))):
        unstack(dq_ref, i, dq.T.astype(jnp.bfloat16))


SMEM = pl.BlockSpec(memory_space=pltpu.SMEM)
VMEM = pl.BlockSpec(memory_space=pltpu.VMEM)
ANY = pl.BlockSpec(memory_space=pl.ANY)


def shape(*dims, dtype=jnp.bfloat16):
    return jax.ShapeDtypeStruct(dims, dtype)


def kernel(body, name, ins, outs, out_specs, scratch, flops, size):
    return pl.pallas_call(
        body,
        out_shape=outs,
        in_specs=ins,
        out_specs=out_specs,
        scratch_shapes=scratch,
        compiler_params=pltpu.CompilerParams(vmem_limit_bytes=48 * 1024 * 1024),
        cost_estimate=pl.CostEstimate(flops=flops, bytes_accessed=size, transcendentals=0),
        name=name,
    )


def per_device(queries, key_rows, value_rows, grad_output, doc_lengths, block_order):
    tokens = queries.shape[0]
    f32, i32, bf16 = jnp.float32, jnp.int32, jnp.bfloat16
    plane = HALF * BLK
    padded = pltpu.VMEM((plane, 2 * HD), bf16)
    scores = pltpu.VMEM((2, LIST * BLK, LANES), f32)
    sem = pltpu.SemaphoreType.DMA
    kv = jnp.concatenate([key_rows, value_rows], axis=1)
    line = lax.all_gather(kv, "ctx", axis=0, tiled=True, axis_index_groups=FIRST)
    spread = jnp.broadcast_to(line[None], (SIDE,) + line.shape)
    own = lax.all_to_all(spread, "ctx", 0, 0, tiled=True, axis_index_groups=SECOND)
    own = own.reshape(plane, 2 * HD)
    oth = lax.ppermute(own, "ctx", SWAP)
    wide = shape(2, HD, LANES, dtype=f32)
    small = shape(4, LANES, dtype=f32)
    meta, vec, stat, part = kernel(
        first_pass,
        "forward_own",
        [SMEM, SMEM, VMEM, ANY],
        (shape(META, dtype=i32), shape(4, LANES, dtype=i32), small, wide),
        (SMEM, VMEM, VMEM, VMEM),
        [padded, pltpu.SMEM((NBLK,), i32), sem],
        2 * 10**9,
        4 * 10**6,
    )(block_order, doc_lengths, queries, own)
    attention, lse, dq, dkv_oth = kernel(
        second_pass,
        "other_plane",
        [SMEM, VMEM, VMEM, VMEM, VMEM, VMEM, ANY],
        (shape(tokens, 2 * HD), small, wide, shape(plane, 2 * HD)),
        (VMEM,) * 4,
        [padded, scores, pltpu.VMEM((2, LIST * BLK, LANES), bf16), sem],
        4 * 10**9,
        6 * 10**6,
    )(meta, vec, stat, queries, grad_output, part, oth)
    back = lax.ppermute(dkv_oth, "ctx", SWAP)
    grad_queries, dkv_own = kernel(
        third_pass,
        "backward_own",
        [SMEM, VMEM, VMEM, VMEM, VMEM, VMEM, ANY],
        (shape(tokens, 2 * HD), shape(plane, 2 * HD)),
        (VMEM,) * 2,
        [padded, sem],
        3 * 10**9,
        6 * 10**6,
    )(meta, vec, lse, queries, grad_output, dq, own)
    part = (dkv_own.astype(f32) + back.astype(f32)).astype(bf16)
    part = part.reshape(SIDE, SIDE * tokens, 2 * HD)
    part = lax.all_to_all(part, "ctx", 0, 0, tiled=True, axis_index_groups=SECOND)
    part = jnp.sum(part.astype(f32), axis=0).astype(bf16).reshape(SIDE, tokens, 2 * HD)
    part = lax.all_to_all(part, "ctx", 0, 0, tiled=True, axis_index_groups=FIRST)
    part = jnp.sum(part.astype(f32), axis=0).astype(bf16)
    return attention, grad_queries, part[:, :HD], part[:, HD:]


def solution(mesh):
    rows = P(("dp", "ctx"), None)
    return jax.shard_map(
        per_device,
        mesh=mesh,
        in_specs=(rows, rows, rows, rows, P("dp"), P("dp")),
        out_specs=(rows, rows, rows, rows),
        check_vma=False,
    )
```

```python
import jax
import jax.numpy as jnp
from jax import lax
from jax.experimental import pallas as pl
from jax.experimental.pallas import tpu as pltpu
from jax.sharding import PartitionSpec as P

BLK = 128
HD = 128
NBLK = 64
NDOC = 16
SIDE = 4
HALF = NBLK // 2
CHUNK = 4
REACH = 17
LIST = 24
ROWS_AT = 4 * LIST
COUNT_AT = 8 * LIST
META = 256
NEG = -1e30
SCALE = HD**-0.5
SCALE2 = SCALE * 1.4426950408889634
LANES = 2 * BLK
LIFT = 4096.0

NT = (((1,), (1,)), ((), ()))
NN = (((1,), (0,)), ((), ()))
TN = (((0,), (0,)), ((), ()))
KEYS, VALS = slice(0, HD), slice(HD, 2 * HD)


def device_of(y, x, core):
    return (y % SIDE) * 2 * SIDE + (x % SIDE) * 2 + core


def along(axis_of_core):
    groups = []
    for core in range(2):
        for fixed in range(SIDE):
            if axis_of_core[core] == "y":
                groups.append([device_of(i, fixed, core) for i in range(SIDE)])
            else:
                groups.append([device_of(fixed, i, core) for i in range(SIDE)])
    return groups


FIRST = along("yx")
SECOND = along("xy")
SWAP = [(i, i ^ 1) for i in range(2 * SIDE * SIDE)]


def mm(a, b, dims):
    return lax.dot_general(a, b, dims, preferred_element_type=jnp.float32)


def stacked(ref, i):
    rows = pl.ds(i * BLK, BLK)
    return jnp.concatenate([ref[rows, :HD], ref[rows, HD:]], axis=0)


def unstack(ref, i, value):
    rows = pl.ds(i * BLK, BLK)
    ref[rows, :HD] = value[:BLK]
    ref[rows, HD:] = value[BLK:]


def place(meta, base, n):
    return pl.multiple_of(meta[ROWS_AT + base + n] * BLK, BLK)


def load(kv, meta, base, t, cols):
    return jnp.concatenate(
        [kv[pl.ds(place(meta, base, t * CHUNK + j), BLK), cols] for j in range(CHUNK)], axis=0
    )


def chunk_at(t):
    return pl.ds(pl.multiple_of(t * CHUNK * BLK, CHUNK * BLK), CHUNK * BLK)


def scores_of(keys, qs, meta, vec, i, base, t):
    s = mm(keys, qs, NT)
    sub = lax.broadcasted_iota(jnp.int32, (BLK, LANES), 0)
    qstart, qpos = vec[2 * i : 2 * i + 1, :], vec[2 * i + 1 : 2 * i + 2, :]
    parts = []
    for j in range(CHUNK):
        first = meta[base + t * CHUNK + j] * BLK
        ok = (sub >= qstart - first) & (sub <= qpos - first)
        parts.append(jnp.where(ok, s[j * BLK : (j + 1) * BLK], NEG))
    return jnp.concatenate(parts, axis=0)


def trips_of(meta, plane):
    most = jnp.maximum(meta[COUNT_AT + plane], meta[COUNT_AT + 2 + plane])
    return (most + CHUNK - 1) // CHUNK


def tops(s):
    return jnp.max(s, axis=0, keepdims=True)


def first_pass(order, lengths, q_ref, own_hbm, meta, vec, stat, part, kv, table, sem):
    copy = fetch_all(own_hbm, kv, sem)
    me = lax.axis_index("ctx")
    core = me & 1
    for s in range(NBLK):
        dev = s // 2
        y, x, c = dev // (2 * SIDE), (dev // 2) % SIDE, dev % 2
        slot = (y * SIDE + x if c else x * SIDE + y) * 2 + s % 2
        table[order[s]] = slot + (HALF * (1 - core) if c else HALF * core)
    lane = lax.broadcasted_iota(jnp.int32, (1, LANES), 1) & (BLK - 1)
    for i in range(2):
        blk = order[2 * me + i]
        qpos = blk * BLK + lane
        end, low = jnp.int32(0), jnp.int32(0)
        qstart = jnp.zeros((1, LANES), jnp.int32)
        for d in range(NDOC):
            end = end + lengths[d]
            qstart = jnp.where(qpos >= end, end, qstart)
            low = jnp.where(blk * BLK >= end, end, low)
        vec[2 * i : 2 * i + 1, :] = qstart
        vec[2 * i + 1 : 2 * i + 2, :] = qpos
        low = low >> 7
        for j in range(2 * LIST):
            meta[2 * i * LIST + j] = -1024
            meta[ROWS_AT + 2 * i * LIST + j] = 0
        mine, others = jnp.int32(2 * i * LIST), jnp.int32((2 * i + 1) * LIST)
        for j in range(REACH):
            p = blk - j
            slot = table[jnp.maximum(p, 0)]
            away = slot >= HALF
            at = jnp.where(away, others, mine)
            meta[at] = p
            meta[ROWS_AT + at] = slot & (HALF - 1)
            step = jnp.where(p >= low, 1, 0)
            others = others + jnp.where(away, step, 0)
            mine = mine + jnp.where(away, 0, step)
        meta[COUNT_AT + 2 * i] = mine - 2 * i * LIST
        meta[COUNT_AT + 2 * i + 1] = others - (2 * i + 1) * LIST
        meta[mine] = -1024
        meta[others] = -1024
    copy.wait()
    qs = [stacked(q_ref, i) for i in range(2)]

    def step(t, carry):
        after = []
        for i in range(2):
            top, total, out = carry[i]
            base = 2 * i * LIST
            s = scores_of(load(kv, meta, base, t, KEYS), qs[i], meta, vec, i, base, t)
            new = jnp.maximum(top, tops(s))
            shrink = jnp.exp2((top - new) * SCALE2)
            p = jnp.exp2((s - new) * SCALE2)
            total = total * shrink + jnp.sum(p, axis=0, keepdims=True)
            out = out * shrink + mm(load(kv, meta, base, t, VALS), p.astype(jnp.bfloat16), TN)
            after.append((new, total, out))
        return tuple(after)

    empty = (
        jnp.full((1, LANES), NEG, jnp.float32),
        jnp.zeros((1, LANES), jnp.float32),
        jnp.zeros((HD, LANES), jnp.float32),
    )
    for i, (top, total, out) in enumerate(lax.fori_loop(0, trips_of(meta, 0), step, (empty, empty))):
        stat[2 * i : 2 * i + 1, :] = top
        stat[2 * i + 1 : 2 * i + 2, :] = total
        part[i] = out


def fetch_all(hbm, kv, sem):
    copy = pltpu.make_async_copy(hbm, kv, sem)
    copy.start()
    return copy


def put(ref, meta, base, t, dk, dv):
    for j in range(CHUNK):
        to = pl.ds(place(meta, base, t * CHUNK + j), BLK)
        rows = slice(j * BLK, (j + 1) * BLK)
        ref[to, KEYS] = (ref[to, KEYS].astype(jnp.float32) + dk[rows]).astype(jnp.bfloat16)
        ref[to, VALS] = (ref[to, VALS].astype(jnp.float32) + dv[rows]).astype(jnp.bfloat16)


def second_pass(meta, vec, stat, q_ref, g_ref, part, oth_hbm, o_ref, lse, dq_ref, dkv, kv, s_ref, p_ref, sem):
    copy = fetch_all(oth_hbm, kv, sem)
    dkv[...] = jnp.zeros_like(dkv)
    copy.wait()
    both = range(2)
    qs, gs = [stacked(q_ref, i) for i in both], [stacked(g_ref, i) for i in both]
    base = [(2 * i + 1) * LIST for i in both]
    trips = trips_of(meta, 1)
    old_top = [stat[2 * i : 2 * i + 1, :] for i in both]

    def scores(t, tops_so_far):
        after = []
        for i in both:
            s = scores_of(load(kv, meta, base[i], t, KEYS), qs[i], meta, vec, i, base[i], t)
            s_ref[i, chunk_at(t), :] = s
            after.append(jnp.maximum(tops_so_far[i], tops(s)))
        return tuple(after)

    top = lax.fori_loop(0, trips, scores, tuple(old_top))

    def outputs(t, carry):
        after = []
        for i in both:
            total, out = carry[i]
            p = jnp.exp2((s_ref[i, chunk_at(t), :] - top[i]) * SCALE2)
            total = total + jnp.sum(p, axis=0, keepdims=True)
            p = p.astype(jnp.bfloat16)
            p_ref[i, chunk_at(t), :] = p
            after.append((total, out + mm(load(kv, meta, base[i], t, VALS), p, TN)))
        return tuple(after)

    start = []
    for i in both:
        shrink = jnp.exp2((old_top[i] - top[i]) * SCALE2)
        start.append((stat[2 * i + 1 : 2 * i + 2, :] * shrink, part[i] * shrink))
    done = lax.fori_loop(0, trips, outputs, tuple(start))
    scaled, delta, over = [], [], []
    for i in both:
        total, out = done[i]
        inv = 1.0 / total
        att = (out * inv).T.astype(jnp.bfloat16)
        unstack(o_ref, i, att)
        wide = gs[i].astype(jnp.float32)
        delta.append(jnp.sum((wide * att.astype(jnp.float32)).T, axis=0, keepdims=True))
        lse[2 * i : 2 * i + 1, :] = top[i] * SCALE2 + jnp.log2(total)
        lse[2 * i + 1 : 2 * i + 2, :] = delta[i]
        scaled.append(inv * SCALE)
        over.append((wide * jnp.broadcast_to(inv, (HD, LANES)).T).astype(jnp.bfloat16))

    def grads(t, dq):
        after = []
        for i in both:
            p = p_ref[i, chunk_at(t), :]
            dp = mm(load(kv, meta, base[i], t, VALS), gs[i], NT)
            ds = ((p.astype(jnp.float32) * scaled[i]) * (dp - delta[i])).astype(jnp.bfloat16)
            put(dkv, meta, base[i], t, mm(ds, qs[i], NN), mm(p, over[i], NN))
            after.append(dq[i] + mm(load(kv, meta, base[i], t, KEYS), ds, TN))
        return tuple(after)

    zero = jnp.zeros((HD, LANES), jnp.float32)
    dq_ref[0], dq_ref[1] = lax.fori_loop(0, trips, grads, (zero, zero))


def third_pass(meta, vec, lse, q_ref, g_ref, dq_in, own_hbm, dq_ref, dkv, kv, sem):
    copy = fetch_all(own_hbm, kv, sem)
    dkv[...] = jnp.zeros_like(dkv)
    copy.wait()
    both = range(2)
    qs, gs = [stacked(q_ref, i) for i in both], [stacked(g_ref, i) for i in both]

    def grads(t, dq):
        after = []
        for i in both:
            base = 2 * i * LIST
            keys = load(kv, meta, base, t, KEYS)
            s = scores_of(keys, qs[i], meta, vec, i, base, t)
            p = jnp.exp2(s * SCALE2 - lse[2 * i : 2 * i + 1, :])
            dp = mm(load(kv, meta, base, t, VALS), gs[i], NT)
            ds = ((p * SCALE) * (dp - lse[2 * i + 1 : 2 * i + 2, :])).astype(jnp.bfloat16)
            put(dkv, meta, base, t, mm(ds, qs[i], NN), mm(p.astype(jnp.bfloat16), gs[i], NN))
            after.append(dq[i] + mm(keys, ds, TN))
        return tuple(after)

    for i, dq in enumerate(lax.fori_loop(0, trips_of(meta, 0), grads, (dq_in[0], dq_in[1]))):
        unstack(dq_ref, i, dq.T.astype(jnp.bfloat16))


SMEM = pl.BlockSpec(memory_space=pltpu.SMEM)
VMEM = pl.BlockSpec(memory_space=pltpu.VMEM)
ANY = pl.BlockSpec(memory_space=pl.ANY)


def shape(*dims, dtype=jnp.bfloat16):
    return jax.ShapeDtypeStruct(dims, dtype)


def kernel(body, name, ins, outs, out_specs, scratch, flops, size):
    return pl.pallas_call(
        body,
        out_shape=outs,
        in_specs=ins,
        out_specs=out_specs,
        scratch_shapes=scratch,
        compiler_params=pltpu.CompilerParams(vmem_limit_bytes=48 * 1024 * 1024),
        cost_estimate=pl.CostEstimate(flops=flops, bytes_accessed=size, transcendentals=0),
        name=name,
    )


def per_device(queries, key_rows, value_rows, grad_output, doc_lengths, block_order):
    tokens = queries.shape[0]
    f32, i32, bf16 = jnp.float32, jnp.int32, jnp.bfloat16
    plane = HALF * BLK
    padded = pltpu.VMEM((plane, 2 * HD), bf16)
    scores = pltpu.VMEM((2, LIST * BLK, LANES), f32)
    sem = pltpu.SemaphoreType.DMA
    kv = jnp.concatenate([key_rows, value_rows], axis=1)
    kv = (kv.astype(f32) * LIFT).astype(jnp.float16)
    line = lax.all_gather(kv, "ctx", axis=0, tiled=True, axis_index_groups=FIRST)
    own = lax.all_gather(line, "ctx", axis=0, tiled=True, axis_index_groups=SECOND)
    own = (own.astype(f32) * (1 / LIFT)).astype(bf16)
    oth = lax.ppermute(own, "ctx", SWAP)
    wide = shape(2, HD, LANES, dtype=f32)
    small = shape(4, LANES, dtype=f32)
    meta, vec, stat, part = kernel(
        first_pass,
        "forward_own",
        [SMEM, SMEM, VMEM, ANY],
        (shape(META, dtype=i32), shape(4, LANES, dtype=i32), small, wide),
        (SMEM, VMEM, VMEM, VMEM),
        [padded, pltpu.SMEM((NBLK,), i32), sem],
        2 * 10**9,
        4 * 10**6,
    )(block_order, doc_lengths, queries, own)
    attention, lse, dq, dkv_oth = kernel(
        second_pass,
        "other_plane",
        [SMEM, VMEM, VMEM, VMEM, VMEM, VMEM, ANY],
        (shape(tokens, 2 * HD), small, wide, shape(plane, 2 * HD)),
        (VMEM,) * 4,
        [padded, scores, pltpu.VMEM((2, LIST * BLK, LANES), bf16), sem],
        4 * 10**9,
        6 * 10**6,
    )(meta, vec, stat, queries, grad_output, part, oth)
    back = lax.ppermute(dkv_oth, "ctx", SWAP)
    grad_queries, dkv_own = kernel(
        third_pass,
        "backward_own",
        [SMEM, VMEM, VMEM, VMEM, VMEM, VMEM, ANY],
        (shape(tokens, 2 * HD), shape(plane, 2 * HD)),
        (VMEM,) * 2,
        [padded, sem],
        3 * 10**9,
        6 * 10**6,
    )(meta, vec, lse, queries, grad_output, dq, own)
    part = (dkv_own.astype(f32) + back.astype(f32)).astype(bf16)
    part = part.reshape(SIDE, SIDE * tokens, 2 * HD)
    part = lax.all_to_all(part, "ctx", 0, 0, tiled=True, axis_index_groups=SECOND)
    part = jnp.sum(part.astype(f32), axis=0).astype(bf16).reshape(SIDE, tokens, 2 * HD)
    part = lax.all_to_all(part, "ctx", 0, 0, tiled=True, axis_index_groups=FIRST)
    part = jnp.sum(part.astype(f32), axis=0).astype(bf16)
    return attention, grad_queries, part[:, :HD], part[:, HD:]


def solution(mesh):
    rows = P(("dp", "ctx"), None)
    return jax.shard_map(
        per_device,
        mesh=mesh,
        in_specs=(rows, rows, rows, rows, P("dp"), P("dp")),
        out_specs=(rows, rows, rows, rows),
        check_vma=False,
    )
```

```python
import jax
import jax.numpy as jnp
from jax import lax
from jax.experimental import pallas as pl
from jax.experimental.pallas import tpu as pltpu
from jax.sharding import PartitionSpec as P

BLK = 128
HD = 128
NBLK = 64
NDOC = 16
SIDE = 4
HALF = NBLK // 2
CHUNK = 4
REACH = 17
LIST = 48
ROWS_AT = 2 * LIST
COUNT_AT = 4 * LIST
META = 256
NEG = -1e30
SCALE = HD**-0.5
SCALE2 = SCALE * 1.4426950408889634
LANES = 2 * BLK
LIFT = 4096.0

NT = (((1,), (1,)), ((), ()))
NN = (((1,), (0,)), ((), ()))
TN = (((0,), (0,)), ((), ()))
KEYS, VALS = slice(0, HD), slice(HD, 2 * HD)


def device_of(y, x, core):
    return (y % SIDE) * 2 * SIDE + (x % SIDE) * 2 + core


def along(axis_of_core):
    groups = []
    for core in range(2):
        for fixed in range(SIDE):
            if axis_of_core[core] == "y":
                groups.append([device_of(i, fixed, core) for i in range(SIDE)])
            else:
                groups.append([device_of(fixed, i, core) for i in range(SIDE)])
    return groups


FIRST = along("yx")
SECOND = along("xy")
SWAP = [(i, i ^ 1) for i in range(2 * SIDE * SIDE)]


def mm(a, b, dims):
    return lax.dot_general(a, b, dims, preferred_element_type=jnp.float32)


def stacked(ref, i):
    rows = pl.ds(i * BLK, BLK)
    return jnp.concatenate([ref[rows, :HD], ref[rows, HD:]], axis=0)


def unstack(ref, i, value):
    rows = pl.ds(i * BLK, BLK)
    ref[rows, :HD] = value[:BLK]
    ref[rows, HD:] = value[BLK:]


def load(kv, meta, plane, ch, cols):
    return jnp.concatenate([kv[pl.ds(row_of(meta, plane, ch, j), BLK), cols] for j in range(CHUNK)], axis=0)


def row_of(meta, plane, ch, j):
    return pl.multiple_of(meta[ROWS_AT + plane * LIST + ch * CHUNK + j] * BLK, BLK)


def scores_of(keys, q, meta, vec, plane, ch, i):
    s = mm(keys, q, NT)
    sub = lax.broadcasted_iota(jnp.int32, (BLK, LANES), 0)
    qstart, qpos = vec[pl.ds(2 * i, 1), :], vec[pl.ds(2 * i + 1, 1), :]
    parts = []
    for j in range(CHUNK):
        first = meta[plane * LIST + ch * CHUNK + j] * BLK
        ok = (sub >= qstart - first) & (sub <= qpos - first)
        parts.append(jnp.where(ok, s[j * BLK : (j + 1) * BLK], NEG))
    return jnp.concatenate(parts, axis=0)


def each_chunk(meta, plane, body):
    split, total = meta[COUNT_AT + 2 * plane], meta[COUNT_AT + 2 * plane + 1]

    def pair(t, _):
        for ch in (2 * t, 2 * t + 1):
            body(ch, jnp.where(ch >= split, 1, 0))
        return 0

    lax.fori_loop(0, total >> 1, pair, 0)

    @pl.when((total & 1) == 1)
    def _():
        body(total - 1, jnp.where(total > split, 1, 0))


def chunk_at(ch):
    return pl.ds(pl.multiple_of(ch * CHUNK * BLK, CHUNK * BLK), CHUNK * BLK)


def forward(meta, vec, plane, kv, q_st, top, total, out, s_ref, p_ref, old_top=None):
    def scores(ch, i):
        s = scores_of(load(kv, meta, plane, ch, KEYS), q_st[i], meta, vec, plane, ch, i)
        s_ref[chunk_at(ch), :] = s
        row = pl.ds(i, 1)
        top[row, :] = jnp.maximum(top[row, :], jnp.max(s, axis=0, keepdims=True))

    each_chunk(meta, plane, scores)
    if old_top is not None:
        for i in range(2):
            row = slice(i, i + 1)
            shrink = jnp.exp2((old_top[i] - top[row, :]) * SCALE2)
            total[row, :] = total[row, :] * shrink
            out[i] = out[i] * shrink

    def outputs(ch, i):
        row = pl.ds(i, 1)
        p = jnp.exp2((s_ref[chunk_at(ch), :] - top[row, :]) * SCALE2)
        total[row, :] = total[row, :] + jnp.sum(p, axis=0, keepdims=True)
        p = p.astype(jnp.bfloat16)
        if p_ref is not None:
            p_ref[chunk_at(ch), :] = p
        out[i] = out[i] + mm(load(kv, meta, plane, ch, VALS), p, TN)

    each_chunk(meta, plane, outputs)


def first_pass(order, lengths, q_ref, own_hbm, meta, vec, stat, part, kv, q_st, s_ref, top, total, table, sem):
    copy = fetch_all(own_hbm, kv, sem)
    me = lax.axis_index("ctx")
    core = me & 1
    for s in range(NBLK):
        dev = s // 2
        y, x, c = dev // (2 * SIDE), (dev // 2) % SIDE, dev % 2
        slot = (y * SIDE + x if c else x * SIDE + y) * 2 + s % 2
        table[order[s]] = slot + (HALF * (1 - core) if c else HALF * core)
    lane = lax.broadcasted_iota(jnp.int32, (1, LANES), 1) & (BLK - 1)
    mine, others = jnp.int32(0), jnp.int32(LIST)
    for i in range(2):
        blk = order[2 * me + i]
        qpos = blk * BLK + lane
        end, low = jnp.int32(0), jnp.int32(0)
        qstart = jnp.zeros((1, LANES), jnp.int32)
        for d in range(NDOC):
            end = end + lengths[d]
            qstart = jnp.where(qpos >= end, end, qstart)
            low = jnp.where(blk * BLK >= end, end, low)
        vec[2 * i : 2 * i + 1, :] = qstart
        vec[2 * i + 1 : 2 * i + 2, :] = qpos
        low = low >> 7
        for j in range(REACH):
            p = blk - j
            slot = table[jnp.maximum(p, 0)]
            away = slot >= HALF
            at = jnp.where(away, others, mine)
            meta[at] = p
            meta[ROWS_AT + at] = slot & (HALF - 1)
            step = jnp.where(p >= low, 1, 0)
            others = others + jnp.where(away, step, 0)
            mine = mine + jnp.where(away, 0, step)
        for j in range(CHUNK - 1):
            for at in (mine, others):
                meta[at + j] = -1024
                meta[ROWS_AT + at + j] = 0
        mine = (mine + CHUNK - 1) // CHUNK * CHUNK
        others = (others + CHUNK - 1) // CHUNK * CHUNK
        meta[COUNT_AT + i] = mine // CHUNK
        meta[COUNT_AT + 2 + i] = (others - LIST) // CHUNK
        q_st[i] = stacked(q_ref, i)
    top[...] = jnp.full_like(top, NEG)
    total[...] = jnp.zeros_like(total)
    part[...] = jnp.zeros_like(part)
    copy.wait()
    forward(meta, vec, 0, kv, q_st, top, total, part, s_ref, None)
    stat[pl.ds(0, 2), :] = top[...]
    stat[pl.ds(2, 2), :] = total[...]


def fetch_all(hbm, kv, sem):
    copy = pltpu.make_async_copy(hbm, kv, sem)
    copy.start()
    return copy


def put(ref, meta, plane, ch, dk, dv):
    for j in range(CHUNK):
        to = pl.ds(row_of(meta, plane, ch, j), BLK)
        rows = slice(j * BLK, (j + 1) * BLK)
        ref[to, KEYS] = (ref[to, KEYS].astype(jnp.float32) + dk[rows]).astype(jnp.bfloat16)
        ref[to, VALS] = (ref[to, VALS].astype(jnp.float32) + dv[rows]).astype(jnp.bfloat16)


def second_pass(
    meta, vec, stat, q_ref, g_ref, part, oth_hbm, o_ref, lse, dq_ref, dkv,
    kv, q_st, g_st, over, s_ref, p_ref, top, total, out, scaled, sem
):
    copy = fetch_all(oth_hbm, kv, sem)
    dkv[...] = jnp.zeros_like(dkv)
    dq_ref[...] = jnp.zeros_like(dq_ref)
    for i in range(2):
        q_st[i], g_st[i] = stacked(q_ref, i), stacked(g_ref, i)
    top[...] = stat[pl.ds(0, 2), :]
    total[...] = stat[pl.ds(2, 2), :]
    out[...] = part[...]
    copy.wait()
    forward(meta, vec, 1, kv, q_st, top, total, out, s_ref, p_ref, [stat[i : i + 1, :] for i in range(2)])
    for i in range(2):
        row = slice(i, i + 1)
        inv = 1.0 / total[row, :]
        att = (out[i] * inv).T.astype(jnp.bfloat16)
        unstack(o_ref, i, att)
        wide = g_st[i].astype(jnp.float32)
        lse[i : i + 1, :] = top[row, :] * SCALE2 + jnp.log2(total[row, :])
        lse[2 + i : 3 + i, :] = jnp.sum((wide * att.astype(jnp.float32)).T, axis=0, keepdims=True)
        scaled[row, :] = inv * SCALE
        over[i] = (wide * jnp.broadcast_to(inv, (HD, LANES)).T).astype(jnp.bfloat16)

    def grads(ch, i):
        p = p_ref[chunk_at(ch), :]
        dp = mm(load(kv, meta, 1, ch, VALS), g_st[i], NT)
        ds = ((p.astype(jnp.float32) * scaled[pl.ds(i, 1), :]) * (dp - lse[pl.ds(2 + i, 1), :])).astype(jnp.bfloat16)
        put(dkv, meta, 1, ch, mm(ds, q_st[i], NN), mm(p, over[i], NN))
        dq_ref[i] = dq_ref[i] + mm(load(kv, meta, 1, ch, KEYS), ds, TN)

    each_chunk(meta, 1, grads)


def third_pass(meta, vec, lse, q_ref, g_ref, dq_in, own_hbm, dq_ref, dkv, kv, q_st, g_st, dq, sem):
    copy = fetch_all(own_hbm, kv, sem)
    dkv[...] = jnp.zeros_like(dkv)
    dq[...] = dq_in[...]
    for i in range(2):
        q_st[i], g_st[i] = stacked(q_ref, i), stacked(g_ref, i)
    copy.wait()

    def grads(ch, i):
        keys = load(kv, meta, 0, ch, KEYS)
        s = scores_of(keys, q_st[i], meta, vec, 0, ch, i)
        p = jnp.exp2(s * SCALE2 - lse[pl.ds(i, 1), :])
        dp = mm(load(kv, meta, 0, ch, VALS), g_st[i], NT)
        ds = ((p * SCALE) * (dp - lse[pl.ds(2 + i, 1), :])).astype(jnp.bfloat16)
        put(dkv, meta, 0, ch, mm(ds, q_st[i], NN), mm(p.astype(jnp.bfloat16), g_st[i], NN))
        dq[i] = dq[i] + mm(keys, ds, TN)

    each_chunk(meta, 0, grads)
    for i in range(2):
        unstack(dq_ref, i, dq[i].T.astype(jnp.bfloat16))


SMEM = pl.BlockSpec(memory_space=pltpu.SMEM)
VMEM = pl.BlockSpec(memory_space=pltpu.VMEM)
ANY = pl.BlockSpec(memory_space=pl.ANY)


def shape(*dims, dtype=jnp.bfloat16):
    return jax.ShapeDtypeStruct(dims, dtype)


def kernel(body, name, ins, outs, out_specs, scratch, flops, size):
    return pl.pallas_call(
        body,
        out_shape=outs,
        in_specs=ins,
        out_specs=out_specs,
        scratch_shapes=scratch,
        compiler_params=pltpu.CompilerParams(vmem_limit_bytes=48 * 1024 * 1024),
        cost_estimate=pl.CostEstimate(flops=flops, bytes_accessed=size, transcendentals=0),
        name=name,
    )


def per_device(queries, key_rows, value_rows, grad_output, doc_lengths, block_order):
    tokens = queries.shape[0]
    f32, i32, bf16 = jnp.float32, jnp.int32, jnp.bfloat16
    plane = HALF * BLK
    padded = pltpu.VMEM((plane, 2 * HD), bf16)
    scores = pltpu.VMEM((LIST * BLK, LANES), f32)
    weights = pltpu.VMEM((LIST * BLK, LANES), bf16)
    rows = pltpu.VMEM((2, LANES, HD), bf16)
    pair = pltpu.VMEM((2, LANES), f32)
    sums = pltpu.VMEM((2, HD, LANES), f32)
    sem = pltpu.SemaphoreType.DMA
    kv = jnp.concatenate([key_rows, value_rows], axis=1)
    kv = (kv.astype(f32) * LIFT).astype(jnp.float16)
    line = lax.all_gather(kv, "ctx", axis=0, tiled=True, axis_index_groups=FIRST)
    own = lax.all_gather(line, "ctx", axis=0, tiled=True, axis_index_groups=SECOND)
    own = (own.astype(f32) * (1 / LIFT)).astype(bf16)
    oth = lax.ppermute(own, "ctx", SWAP)
    wide = shape(2, HD, LANES, dtype=f32)
    small = shape(4, LANES, dtype=f32)
    meta, vec, stat, part = kernel(
        first_pass,
        "forward_own",
        [SMEM, SMEM, VMEM, ANY],
        (shape(META, dtype=i32), shape(4, LANES, dtype=i32), small, wide),
        (SMEM, VMEM, VMEM, VMEM),
        [padded, rows, scores, pair, pair, pltpu.SMEM((NBLK,), i32), sem],
        2 * 10**9,
        4 * 10**6,
    )(block_order, doc_lengths, queries, own)
    attention, lse, dq, dkv_oth = kernel(
        second_pass,
        "other_plane",
        [SMEM, VMEM, VMEM, VMEM, VMEM, VMEM, ANY],
        (shape(tokens, 2 * HD), small, wide, shape(plane, 2 * HD)),
        (VMEM,) * 4,
        [padded, rows, rows, rows, scores, weights, pair, pair, sums, pair, sem],
        4 * 10**9,
        6 * 10**6,
    )(meta, vec, stat, queries, grad_output, part, oth)
    back = lax.ppermute(dkv_oth, "ctx", SWAP)
    grad_queries, dkv_own = kernel(
        third_pass,
        "backward_own",
        [SMEM, VMEM, VMEM, VMEM, VMEM, VMEM, ANY],
        (shape(tokens, 2 * HD), shape(plane, 2 * HD)),
        (VMEM,) * 2,
        [padded, rows, rows, sums, sem],
        3 * 10**9,
        6 * 10**6,
    )(meta, vec, lse, queries, grad_output, dq, own)
    part = (dkv_own.astype(f32) + back.astype(f32)).astype(bf16)
    part = part.reshape(SIDE, SIDE * tokens, 2 * HD)
    part = lax.all_to_all(part, "ctx", 0, 0, tiled=True, axis_index_groups=SECOND)
    part = jnp.sum(part.astype(f32), axis=0).astype(bf16).reshape(SIDE, tokens, 2 * HD)
    part = lax.all_to_all(part, "ctx", 0, 0, tiled=True, axis_index_groups=FIRST)
    part = jnp.sum(part.astype(f32), axis=0).astype(bf16)
    return attention, grad_queries, part[:, :HD], part[:, HD:]


def solution(mesh):
    rows = P(("dp", "ctx"), None)
    return jax.shard_map(
        per_device,
        mesh=mesh,
        in_specs=(rows, rows, rows, rows, P("dp"), P("dp")),
        out_specs=(rows, rows, rows, rows),
        check_vma=False,
    )
```

```python
import jax
import jax.numpy as jnp
from jax import lax
from jax.experimental import pallas as pl
from jax.experimental.pallas import tpu as pltpu
from jax.sharding import PartitionSpec as P

BLK = 128
HD = 128
NBLK = 64
NDOC = 16
SIDE = 4
HALF = NBLK // 2
CHUNK = 4
REACH = 17
LIST = 48
ROWS_AT = 2 * LIST
COUNT_AT = 4 * LIST
META = 256
NEG = -1e30
SCALE = HD**-0.5
SCALE2 = SCALE * 1.4426950408889634
LANES = 2 * BLK
LIFT = 4096.0

NT = (((1,), (1,)), ((), ()))
NN = (((1,), (0,)), ((), ()))
TN = (((0,), (0,)), ((), ()))
KEYS, VALS = slice(0, HD), slice(HD, 2 * HD)


def device_of(y, x, core):
    return (y % SIDE) * 2 * SIDE + (x % SIDE) * 2 + core


def along(axis_of_core):
    groups = []
    for core in range(2):
        for fixed in range(SIDE):
            if axis_of_core[core] == "y":
                groups.append([device_of(i, fixed, core) for i in range(SIDE)])
            else:
                groups.append([device_of(fixed, i, core) for i in range(SIDE)])
    return groups


FIRST = along("yx")
SECOND = along("xy")
SWAP = [(i, i ^ 1) for i in range(2 * SIDE * SIDE)]


def mm(a, b, dims):
    return lax.dot_general(a, b, dims, preferred_element_type=jnp.float32)


def stacked(ref, i):
    rows = pl.ds(i * BLK, BLK)
    return jnp.concatenate([ref[rows, :HD], ref[rows, HD:]], axis=0)


def unstack(ref, i, value):
    rows = pl.ds(i * BLK, BLK)
    ref[rows, :HD] = value[:BLK]
    ref[rows, HD:] = value[BLK:]


def load(kv, meta, plane, ch, cols):
    return jnp.concatenate([kv[pl.ds(row_of(meta, plane, ch, j), BLK), cols] for j in range(CHUNK)], axis=0)


def row_of(meta, plane, ch, j):
    return pl.multiple_of(meta[ROWS_AT + plane * LIST + ch * CHUNK + j] * BLK, BLK)


def scores_of(keys, q, meta, vec, plane, ch, i):
    s = mm(keys, q, NT)
    sub = lax.broadcasted_iota(jnp.int32, (BLK, LANES), 0)
    qstart, qpos = vec[pl.ds(2 * i, 1), :], vec[pl.ds(2 * i + 1, 1), :]
    parts = []
    for j in range(CHUNK):
        first = meta[plane * LIST + ch * CHUNK + j] * BLK
        ok = (sub >= qstart - first) & (sub <= qpos - first)
        parts.append(jnp.where(ok, s[j * BLK : (j + 1) * BLK], NEG))
    return jnp.concatenate(parts, axis=0)


def each_chunk(meta, plane, body):
    split, total = meta[COUNT_AT + 2 * plane], meta[COUNT_AT + 2 * plane + 1]

    def pair(t, _):
        for ch in (2 * t, 2 * t + 1):
            body(ch, jnp.where(ch >= split, 1, 0))
        return 0

    lax.fori_loop(0, total >> 1, pair, 0)

    @pl.when((total & 1) == 1)
    def _():
        body(total - 1, jnp.where(total > split, 1, 0))


def chunk_at(ch):
    return pl.ds(pl.multiple_of(ch * CHUNK * BLK, CHUNK * BLK), CHUNK * BLK)


def forward(meta, vec, plane, kv, q_st, top, total, out, s_ref, p_ref, old_top=None):
    def scores(ch, i):
        s = scores_of(load(kv, meta, plane, ch, KEYS), q_st[i], meta, vec, plane, ch, i)
        s_ref[chunk_at(ch), :] = s
        row = pl.ds(i, 1)
        top[row, :] = jnp.maximum(top[row, :], jnp.max(s, axis=0, keepdims=True))

    each_chunk(meta, plane, scores)
    if old_top is not None:
        for i in range(2):
            row = slice(i, i + 1)
            shrink = jnp.exp2((old_top[i] - top[row, :]) * SCALE2)
            total[row, :] = total[row, :] * shrink
            out[i] = out[i] * shrink

    def outputs(ch, i):
        row = pl.ds(i, 1)
        p = jnp.exp2((s_ref[chunk_at(ch), :] - top[row, :]) * SCALE2)
        total[row, :] = total[row, :] + jnp.sum(p, axis=0, keepdims=True)
        p = p.astype(jnp.bfloat16)
        if p_ref is not None:
            p_ref[chunk_at(ch), :] = p
        out[i] = out[i] + mm(load(kv, meta, plane, ch, VALS), p, TN)

    each_chunk(meta, plane, outputs)


def first_pass(order, lengths, q_ref, kv, meta, vec, stat, part, q_st, s_ref, top, total, table):
    me = lax.axis_index("ctx")
    core = me & 1
    for s in range(NBLK):
        dev = s // 2
        y, x, c = dev // (2 * SIDE), (dev // 2) % SIDE, dev % 2
        slot = (y * SIDE + x if c else x * SIDE + y) * 2 + s % 2
        table[order[s]] = slot + (HALF * (1 - core) if c else HALF * core)
    lane = lax.broadcasted_iota(jnp.int32, (1, LANES), 1) & (BLK - 1)
    mine, others = jnp.int32(0), jnp.int32(LIST)
    for i in range(2):
        blk = order[2 * me + i]
        qpos = blk * BLK + lane
        end, low = jnp.int32(0), jnp.int32(0)
        qstart = jnp.zeros((1, LANES), jnp.int32)
        for d in range(NDOC):
            end = end + lengths[d]
            qstart = jnp.where(qpos >= end, end, qstart)
            low = jnp.where(blk * BLK >= end, end, low)
        vec[2 * i : 2 * i + 1, :] = qstart
        vec[2 * i + 1 : 2 * i + 2, :] = qpos
        low = low >> 7
        for j in range(REACH):
            p = blk - j
            slot = table[jnp.maximum(p, 0)]
            away = slot >= HALF
            at = jnp.where(away, others, mine)
            meta[at] = p
            meta[ROWS_AT + at] = slot & (HALF - 1)
            step = jnp.where(p >= low, 1, 0)
            others = others + jnp.where(away, step, 0)
            mine = mine + jnp.where(away, 0, step)
        for j in range(CHUNK - 1):
            for at in (mine, others):
                meta[at + j] = -1024
                meta[ROWS_AT + at + j] = 0
        mine = (mine + CHUNK - 1) // CHUNK * CHUNK
        others = (others + CHUNK - 1) // CHUNK * CHUNK
        meta[COUNT_AT + i] = mine // CHUNK
        meta[COUNT_AT + 2 + i] = (others - LIST) // CHUNK
        q_st[i] = stacked(q_ref, i)
    top[...] = jnp.full_like(top, NEG)
    total[...] = jnp.zeros_like(total)
    part[...] = jnp.zeros_like(part)
    forward(meta, vec, 0, kv, q_st, top, total, part, s_ref, None)
    stat[pl.ds(0, 2), :] = top[...]
    stat[pl.ds(2, 2), :] = total[...]


def put(ref, meta, plane, ch, dk, dv):
    for j in range(CHUNK):
        to = pl.ds(row_of(meta, plane, ch, j), BLK)
        rows = slice(j * BLK, (j + 1) * BLK)
        ref[to, KEYS] = (ref[to, KEYS].astype(jnp.float32) + dk[rows]).astype(jnp.bfloat16)
        ref[to, VALS] = (ref[to, VALS].astype(jnp.float32) + dv[rows]).astype(jnp.bfloat16)


def second_pass(
    meta, vec, stat, q_ref, g_ref, part, kv, o_ref, lse, dq_ref, dkv,
    q_st, g_st, over, s_ref, p_ref, top, total, out, scaled
):
    dkv[...] = jnp.zeros_like(dkv)
    dq_ref[...] = jnp.zeros_like(dq_ref)
    for i in range(2):
        q_st[i], g_st[i] = stacked(q_ref, i), stacked(g_ref, i)
    top[...] = stat[pl.ds(0, 2), :]
    total[...] = stat[pl.ds(2, 2), :]
    out[...] = part[...]
    forward(meta, vec, 1, kv, q_st, top, total, out, s_ref, p_ref, [stat[i : i + 1, :] for i in range(2)])
    for i in range(2):
        row = slice(i, i + 1)
        inv = 1.0 / total[row, :]
        att = (out[i] * inv).T.astype(jnp.bfloat16)
        unstack(o_ref, i, att)
        wide = g_st[i].astype(jnp.float32)
        lse[i : i + 1, :] = top[row, :] * SCALE2 + jnp.log2(total[row, :])
        lse[2 + i : 3 + i, :] = jnp.sum((wide * att.astype(jnp.float32)).T, axis=0, keepdims=True)
        scaled[row, :] = inv * SCALE
        over[i] = (wide * jnp.broadcast_to(inv, (HD, LANES)).T).astype(jnp.bfloat16)

    def grads(ch, i):
        p = p_ref[chunk_at(ch), :]
        dp = mm(load(kv, meta, 1, ch, VALS), g_st[i], NT)
        ds = ((p.astype(jnp.float32) * scaled[pl.ds(i, 1), :]) * (dp - lse[pl.ds(2 + i, 1), :])).astype(jnp.bfloat16)
        put(dkv, meta, 1, ch, mm(ds, q_st[i], NN), mm(p, over[i], NN))
        dq_ref[i] = dq_ref[i] + mm(load(kv, meta, 1, ch, KEYS), ds, TN)

    each_chunk(meta, 1, grads)


def third_pass(meta, vec, lse, q_ref, g_ref, dq_in, kv, dq_ref, dkv, q_st, g_st, dq):
    dkv[...] = jnp.zeros_like(dkv)
    dq[...] = dq_in[...]
    for i in range(2):
        q_st[i], g_st[i] = stacked(q_ref, i), stacked(g_ref, i)

    def grads(ch, i):
        keys = load(kv, meta, 0, ch, KEYS)
        s = scores_of(keys, q_st[i], meta, vec, 0, ch, i)
        p = jnp.exp2(s * SCALE2 - lse[pl.ds(i, 1), :])
        dp = mm(load(kv, meta, 0, ch, VALS), g_st[i], NT)
        ds = ((p * SCALE) * (dp - lse[pl.ds(2 + i, 1), :])).astype(jnp.bfloat16)
        put(dkv, meta, 0, ch, mm(ds, q_st[i], NN), mm(p.astype(jnp.bfloat16), g_st[i], NN))
        dq[i] = dq[i] + mm(keys, ds, TN)

    each_chunk(meta, 0, grads)
    for i in range(2):
        unstack(dq_ref, i, dq[i].T.astype(jnp.bfloat16))


SMEM = pl.BlockSpec(memory_space=pltpu.SMEM)
VMEM = pl.BlockSpec(memory_space=pltpu.VMEM)


def shape(*dims, dtype=jnp.bfloat16):
    return jax.ShapeDtypeStruct(dims, dtype)


def kernel(body, name, ins, outs, out_specs, scratch, flops, size):
    return pl.pallas_call(
        body,
        out_shape=outs,
        in_specs=ins,
        out_specs=out_specs,
        scratch_shapes=scratch,
        compiler_params=pltpu.CompilerParams(vmem_limit_bytes=24 * 1024 * 1024),
        cost_estimate=pl.CostEstimate(flops=flops, bytes_accessed=size, transcendentals=0),
        name=name,
    )


def per_device(queries, key_rows, value_rows, grad_output, doc_lengths, block_order):
    tokens = queries.shape[0]
    f32, i32, bf16 = jnp.float32, jnp.int32, jnp.bfloat16
    plane = HALF * BLK
    scores = pltpu.VMEM((LIST * BLK, LANES), f32)
    weights = pltpu.VMEM((LIST * BLK, LANES), bf16)
    rows = pltpu.VMEM((2, LANES, HD), bf16)
    pair = pltpu.VMEM((2, LANES), f32)
    sums = pltpu.VMEM((2, HD, LANES), f32)
    kv = jnp.concatenate([key_rows, value_rows], axis=1)
    kv = (kv.astype(f32) * LIFT).astype(jnp.float16)
    line = jnp.broadcast_to(kv[None], (SIDE, tokens, 2 * HD))
    line = lax.all_to_all(line, "ctx", 0, 0, tiled=True, axis_index_groups=FIRST)
    line = line.reshape(SIDE * tokens, 2 * HD)
    own = lax.all_gather(line, "ctx", axis=0, tiled=True, axis_index_groups=SECOND)
    own = (own.astype(f32) * (1 / LIFT)).astype(bf16)
    oth = lax.ppermute(own, "ctx", SWAP)
    wide = shape(2, HD, LANES, dtype=f32)
    small = shape(4, LANES, dtype=f32)
    meta, vec, stat, part = kernel(
        first_pass,
        "forward_own",
        [SMEM, SMEM, VMEM, VMEM],
        (shape(META, dtype=i32), shape(4, LANES, dtype=i32), small, wide),
        (SMEM, VMEM, VMEM, VMEM),
        [rows, scores, pair, pair, pltpu.SMEM((NBLK,), i32)],
        2 * 10**9,
        4 * 10**6,
    )(block_order, doc_lengths, queries, own)
    attention, lse, dq, dkv_oth = kernel(
        second_pass,
        "other_plane",
        [SMEM, VMEM, VMEM, VMEM, VMEM, VMEM, VMEM],
        (shape(tokens, 2 * HD), small, wide, shape(plane, 2 * HD)),
        (VMEM,) * 4,
        [rows, rows, rows, scores, weights, pair, pair, sums, pair],
        4 * 10**9,
        6 * 10**6,
    )(meta, vec, stat, queries, grad_output, part, oth)
    back = lax.ppermute(dkv_oth, "ctx", SWAP)
    grad_queries, dkv_own = kernel(
        third_pass,
        "backward_own",
        [SMEM, VMEM, VMEM, VMEM, VMEM, VMEM, VMEM],
        (shape(tokens, 2 * HD), shape(plane, 2 * HD)),
        (VMEM,) * 2,
        [rows, rows, sums],
        3 * 10**9,
        6 * 10**6,
    )(meta, vec, lse, queries, grad_output, dq, own)
    part = (dkv_own.astype(f32) + back.astype(f32)).astype(bf16)
    part = part.reshape(SIDE, SIDE * tokens, 2 * HD)
    part = lax.all_to_all(part, "ctx", 0, 0, tiled=True, axis_index_groups=SECOND)
    part = jnp.sum(part.astype(f32), axis=0).astype(bf16).reshape(SIDE, tokens, 2 * HD)
    part = lax.all_to_all(part, "ctx", 0, 0, tiled=True, axis_index_groups=FIRST)
    part = jnp.sum(part.astype(f32), axis=0).astype(bf16)
    return attention, grad_queries, part[:, :HD], part[:, HD:]


def solution(mesh):
    rows = P(("dp", "ctx"), None)
    return jax.shard_map(
        per_device,
        mesh=mesh,
        in_specs=(rows, rows, rows, rows, P("dp"), P("dp")),
        out_specs=(rows, rows, rows, rows),
        check_vma=False,
    )
```

```python
import jax
import jax.numpy as jnp
from jax import lax
from jax.experimental import pallas as pl
from jax.experimental.pallas import tpu as pltpu
from jax.sharding import PartitionSpec as P

BLK = 128
HD = 128
NBLK = 64
NDOC = 16
SIDE = 4
HALF = NBLK // 2
CHUNK = 4
REACH = 17
LIST = 48
ROWS_AT = 2 * LIST
COUNT_AT = 4 * LIST
META = 256
NEG = -1e30
SCALE = HD**-0.5
SCALE2 = SCALE * 1.4426950408889634
LANES = 2 * BLK
LIFT = 4096.0

NT = (((1,), (1,)), ((), ()))
NN = (((1,), (0,)), ((), ()))
TN = (((0,), (0,)), ((), ()))
KEYS, VALS = slice(0, HD), slice(HD, 2 * HD)


def device_of(y, x, core):
    return (y % SIDE) * 2 * SIDE + (x % SIDE) * 2 + core


def along(axis_of_core):
    groups = []
    for core in range(2):
        for fixed in range(SIDE):
            if axis_of_core[core] == "y":
                groups.append([device_of(i, fixed, core) for i in range(SIDE)])
            else:
                groups.append([device_of(fixed, i, core) for i in range(SIDE)])
    return groups


FIRST = along("yx")
SECOND = along("xy")
SWAP = [(i, i ^ 1) for i in range(2 * SIDE * SIDE)]


def mm(a, b, dims):
    return lax.dot_general(a, b, dims, preferred_element_type=jnp.float32)


def stacked(ref, i):
    rows = pl.ds(i * BLK, BLK)
    return jnp.concatenate([ref[rows, :HD], ref[rows, HD:]], axis=0)


def unstack(ref, i, value):
    rows = pl.ds(i * BLK, BLK)
    ref[rows, :HD] = value[:BLK]
    ref[rows, HD:] = value[BLK:]


def load(kv, meta, plane, ch, cols):
    return jnp.concatenate([kv[pl.ds(row_of(meta, plane, ch, j), BLK), cols] for j in range(CHUNK)], axis=0)


def row_of(meta, plane, ch, j):
    return pl.multiple_of(meta[ROWS_AT + plane * LIST + ch * CHUNK + j] * BLK, BLK)


def scores_of(keys, q, meta, vec, plane, ch, i):
    s = mm(keys, q, NT)
    sub = lax.broadcasted_iota(jnp.int32, (BLK, LANES), 0)
    qstart, qpos = vec[pl.ds(2 * i, 1), :], vec[pl.ds(2 * i + 1, 1), :]
    parts = []
    for j in range(CHUNK):
        first = meta[plane * LIST + ch * CHUNK + j] * BLK
        ok = (sub >= qstart - first) & (sub <= qpos - first)
        parts.append(jnp.where(ok, s[j * BLK : (j + 1) * BLK], NEG))
    return jnp.concatenate(parts, axis=0)


def each_chunk(meta, plane, body):
    split, total = meta[COUNT_AT + 2 * plane], meta[COUNT_AT + 2 * plane + 1]

    def pair(t, _):
        for ch in (2 * t, 2 * t + 1):
            body(ch, jnp.where(ch >= split, 1, 0))
        return 0

    lax.fori_loop(0, total >> 1, pair, 0)

    @pl.when((total & 1) == 1)
    def _():
        body(total - 1, jnp.where(total > split, 1, 0))


def chunk_at(ch):
    return pl.ds(pl.multiple_of(ch * CHUNK * BLK, CHUNK * BLK), CHUNK * BLK)


def forward(meta, vec, plane, kv, q_st, top, total, out, s_ref, p_ref, old_top=None):
    def scores(ch, i):
        s = scores_of(load(kv, meta, plane, ch, KEYS), q_st[i], meta, vec, plane, ch, i)
        s_ref[chunk_at(ch), :] = s
        row = pl.ds(i, 1)
        top[row, :] = jnp.maximum(top[row, :], jnp.max(s, axis=0, keepdims=True))

    each_chunk(meta, plane, scores)
    if old_top is not None:
        for i in range(2):
            row = slice(i, i + 1)
            shrink = jnp.exp2((old_top[i] - top[row, :]) * SCALE2)
            total[row, :] = total[row, :] * shrink
            out[i] = out[i] * shrink

    def outputs(ch, i):
        row = pl.ds(i, 1)
        p = jnp.exp2((s_ref[chunk_at(ch), :] - top[row, :]) * SCALE2)
        total[row, :] = total[row, :] + jnp.sum(p, axis=0, keepdims=True)
        p = p.astype(jnp.bfloat16)
        if p_ref is not None:
            p_ref[chunk_at(ch), :] = p
        out[i] = out[i] + mm(load(kv, meta, plane, ch, VALS), p, TN)

    each_chunk(meta, plane, outputs)


def first_pass(order, lengths, q_ref, kv, meta, vec, stat, part, q_st, s_ref, top, total, table):
    me = lax.axis_index("ctx")
    core = me & 1
    for s in range(NBLK):
        dev = s // 2
        y, x, c = dev // (2 * SIDE), (dev // 2) % SIDE, dev % 2
        slot = (y * SIDE + x if c else x * SIDE + y) * 2 + s % 2
        table[order[s]] = slot + (HALF * (1 - core) if c else HALF * core)
    lane = lax.broadcasted_iota(jnp.int32, (1, LANES), 1) & (BLK - 1)
    mine, others = jnp.int32(0), jnp.int32(LIST)
    for i in range(2):
        blk = order[2 * me + i]
        qpos = blk * BLK + lane
        end, low = jnp.int32(0), jnp.int32(0)
        qstart = jnp.zeros((1, LANES), jnp.int32)
        for d in range(NDOC):
            end = end + lengths[d]
            qstart = jnp.where(qpos >= end, end, qstart)
            low = jnp.where(blk * BLK >= end, end, low)
        vec[2 * i : 2 * i + 1, :] = qstart
        vec[2 * i + 1 : 2 * i + 2, :] = qpos
        low = low >> 7
        for j in range(REACH):
            p = blk - j
            slot = table[jnp.maximum(p, 0)]
            away = slot >= HALF
            at = jnp.where(away, others, mine)
            meta[at] = p
            meta[ROWS_AT + at] = slot & (HALF - 1)
            step = jnp.where(p >= low, 1, 0)
            others = others + jnp.where(away, step, 0)
            mine = mine + jnp.where(away, 0, step)
        for j in range(CHUNK - 1):
            for at in (mine, others):
                meta[at + j] = -1024
                meta[ROWS_AT + at + j] = 0
        mine = (mine + CHUNK - 1) // CHUNK * CHUNK
        others = (others + CHUNK - 1) // CHUNK * CHUNK
        meta[COUNT_AT + i] = mine // CHUNK
        meta[COUNT_AT + 2 + i] = (others - LIST) // CHUNK
        q_st[i] = stacked(q_ref, i)
    top[...] = jnp.full_like(top, NEG)
    total[...] = jnp.zeros_like(total)
    part[...] = jnp.zeros_like(part)
    forward(meta, vec, 0, kv, q_st, top, total, part, s_ref, None)
    stat[pl.ds(0, 2), :] = top[...]
    stat[pl.ds(2, 2), :] = total[...]


def put(ref, meta, plane, ch, dk, dv):
    for j in range(CHUNK):
        to = pl.ds(row_of(meta, plane, ch, j), BLK)
        rows = slice(j * BLK, (j + 1) * BLK)
        ref[to, KEYS] = (ref[to, KEYS].astype(jnp.float32) + dk[rows]).astype(jnp.bfloat16)
        ref[to, VALS] = (ref[to, VALS].astype(jnp.float32) + dv[rows]).astype(jnp.bfloat16)


def second_pass(
    meta, vec, stat, q_ref, g_ref, part, kv, o_ref, lse, dq_ref, dkv,
    q_st, g_st, over, s_ref, p_ref, top, total, out, scaled
):
    dkv[...] = jnp.zeros_like(dkv)
    dq_ref[...] = jnp.zeros_like(dq_ref)
    for i in range(2):
        q_st[i], g_st[i] = stacked(q_ref, i), stacked(g_ref, i)
    top[...] = stat[pl.ds(0, 2), :]
    total[...] = stat[pl.ds(2, 2), :]
    out[...] = part[...]
    forward(meta, vec, 1, kv, q_st, top, total, out, s_ref, p_ref, [stat[i : i + 1, :] for i in range(2)])
    for i in range(2):
        row = slice(i, i + 1)
        inv = 1.0 / total[row, :]
        att = (out[i] * inv).T.astype(jnp.bfloat16)
        unstack(o_ref, i, att)
        wide = g_st[i].astype(jnp.float32)
        lse[i : i + 1, :] = top[row, :] * SCALE2 + jnp.log2(total[row, :])
        lse[2 + i : 3 + i, :] = jnp.sum((wide * att.astype(jnp.float32)).T, axis=0, keepdims=True)
        scaled[row, :] = inv * SCALE
        over[i] = (wide * jnp.broadcast_to(inv, (HD, LANES)).T).astype(jnp.bfloat16)

    def grads(ch, i):
        p = p_ref[chunk_at(ch), :]
        dp = mm(load(kv, meta, 1, ch, VALS), g_st[i], NT)
        ds = ((p.astype(jnp.float32) * scaled[pl.ds(i, 1), :]) * (dp - lse[pl.ds(2 + i, 1), :])).astype(jnp.bfloat16)
        put(dkv, meta, 1, ch, mm(ds, q_st[i], NN), mm(p, over[i], NN))
        dq_ref[i] = dq_ref[i] + mm(load(kv, meta, 1, ch, KEYS), ds, TN)

    each_chunk(meta, 1, grads)


def third_pass(meta, vec, lse, q_ref, g_ref, dq_in, att_in, kv, o_ref, dq_ref, dkv, q_st, g_st, dq):
    o_ref[...] = att_in[...]
    dkv[...] = jnp.zeros_like(dkv)
    dq[...] = dq_in[...]
    for i in range(2):
        q_st[i], g_st[i] = stacked(q_ref, i), stacked(g_ref, i)

    def grads(ch, i):
        keys = load(kv, meta, 0, ch, KEYS)
        s = scores_of(keys, q_st[i], meta, vec, 0, ch, i)
        p = jnp.exp2(s * SCALE2 - lse[pl.ds(i, 1), :])
        dp = mm(load(kv, meta, 0, ch, VALS), g_st[i], NT)
        ds = ((p * SCALE) * (dp - lse[pl.ds(2 + i, 1), :])).astype(jnp.bfloat16)
        put(dkv, meta, 0, ch, mm(ds, q_st[i], NN), mm(p.astype(jnp.bfloat16), g_st[i], NN))
        dq[i] = dq[i] + mm(keys, ds, TN)

    each_chunk(meta, 0, grads)
    for i in range(2):
        unstack(dq_ref, i, dq[i].T.astype(jnp.bfloat16))


SMEM = pl.BlockSpec(memory_space=pltpu.SMEM)
VMEM = pl.BlockSpec(memory_space=pltpu.VMEM)


def shape(*dims, dtype=jnp.bfloat16):
    return jax.ShapeDtypeStruct(dims, dtype)


def kernel(body, name, ins, outs, out_specs, scratch, flops, size):
    return pl.pallas_call(
        body,
        out_shape=outs,
        in_specs=ins,
        out_specs=out_specs,
        scratch_shapes=scratch,
        compiler_params=pltpu.CompilerParams(vmem_limit_bytes=24 * 1024 * 1024),
        cost_estimate=pl.CostEstimate(flops=flops, bytes_accessed=size, transcendentals=0),
        name=name,
    )


def per_device(queries, key_rows, value_rows, grad_output, doc_lengths, block_order):
    tokens = queries.shape[0]
    f32, i32, bf16 = jnp.float32, jnp.int32, jnp.bfloat16
    plane = HALF * BLK
    scores = pltpu.VMEM((LIST * BLK, LANES), f32)
    weights = pltpu.VMEM((LIST * BLK, LANES), bf16)
    rows = pltpu.VMEM((2, LANES, HD), bf16)
    pair = pltpu.VMEM((2, LANES), f32)
    sums = pltpu.VMEM((2, HD, LANES), f32)
    kv = jnp.concatenate([key_rows, value_rows], axis=1)
    kv = (kv.astype(f32) * LIFT).astype(jnp.float16)
    line = jnp.broadcast_to(kv[None], (SIDE, tokens, 2 * HD))
    line = lax.all_to_all(line, "ctx", 0, 0, tiled=True, axis_index_groups=FIRST)
    line = line.reshape(SIDE * tokens, 2 * HD)
    own = lax.all_gather(line, "ctx", axis=0, tiled=True, axis_index_groups=SECOND)
    own = (own.astype(f32) * (1 / LIFT)).astype(bf16)
    oth = lax.ppermute(own, "ctx", SWAP)
    wide = shape(2, HD, LANES, dtype=f32)
    small = shape(4, LANES, dtype=f32)
    meta, vec, stat, part = kernel(
        first_pass,
        "forward_own",
        [SMEM, SMEM, VMEM, VMEM],
        (shape(META, dtype=i32), shape(4, LANES, dtype=i32), small, wide),
        (SMEM, VMEM, VMEM, VMEM),
        [rows, scores, pair, pair, pltpu.SMEM((NBLK,), i32)],
        2 * 10**9,
        4 * 10**6,
    )(block_order, doc_lengths, queries, own)
    att, lse, dq, dkv_oth = kernel(
        second_pass,
        "other_plane",
        [SMEM, VMEM, VMEM, VMEM, VMEM, VMEM, VMEM],
        (shape(tokens, 2 * HD), small, wide, shape(plane, 2 * HD)),
        (VMEM,) * 4,
        [rows, rows, rows, scores, weights, pair, pair, sums, pair],
        4 * 10**9,
        6 * 10**6,
    )(meta, vec, stat, queries, grad_output, part, oth)
    back = lax.ppermute(dkv_oth, "ctx", SWAP)
    attention, grad_queries, dkv_own = kernel(
        third_pass,
        "backward_own",
        [SMEM, VMEM, VMEM, VMEM, VMEM, VMEM, VMEM, VMEM],
        (shape(tokens, 2 * HD), shape(tokens, 2 * HD), shape(plane, 2 * HD)),
        (VMEM,) * 3,
        [rows, rows, sums],
        3 * 10**9,
        6 * 10**6,
    )(meta, vec, lse, queries, grad_output, dq, att, own)
    part = (dkv_own.astype(f32) + back.astype(f32)).astype(bf16)
    part = part.reshape(SIDE, SIDE * tokens, 2 * HD)
    part = lax.all_to_all(part, "ctx", 0, 0, tiled=True, axis_index_groups=SECOND)
    part = jnp.sum(part.astype(f32), axis=0).astype(bf16).reshape(SIDE, tokens, 2 * HD)
    part = lax.all_to_all(part, "ctx", 0, 0, tiled=True, axis_index_groups=FIRST)
    part = jnp.sum(part.astype(f32), axis=0).astype(bf16)
    return attention, grad_queries, part[:, :HD], part[:, HD:]


def solution(mesh):
    rows = P(("dp", "ctx"), None)
    return jax.shard_map(
        per_device,
        mesh=mesh,
        in_specs=(rows, rows, rows, rows, P("dp"), P("dp")),
        out_specs=(rows, rows, rows, rows),
        check_vma=False,
    )
```

```python
import jax
import jax.numpy as jnp
from jax import lax
from jax.experimental import pallas as pl
from jax.experimental.pallas import tpu as pltpu
from jax.sharding import PartitionSpec as P

BLK = 128
HD = 128
NBLK = 64
NDOC = 16
SIDE = 4
HALF = NBLK // 2
CHUNK = 4
REACH = 17
LIST = 48
ROWS_AT = 2 * LIST
COUNT_AT = 4 * LIST
META = 256
NEG = -1e30
SCALE = HD**-0.5
SCALE2 = SCALE * 1.4426950408889634
LANES = 2 * BLK
LIFT = 4096.0

NT = (((1,), (1,)), ((), ()))
NN = (((1,), (0,)), ((), ()))
TN = (((0,), (0,)), ((), ()))
KEYS, VALS = slice(0, HD), slice(HD, 2 * HD)


def device_of(y, x, core):
    return (y % SIDE) * 2 * SIDE + (x % SIDE) * 2 + core


def along(axis_of_core):
    groups = []
    for core in range(2):
        for fixed in range(SIDE):
            if axis_of_core[core] == "y":
                groups.append([device_of(i, fixed, core) for i in range(SIDE)])
            else:
                groups.append([device_of(fixed, i, core) for i in range(SIDE)])
    return groups


FIRST = along("yx")
SECOND = along("xy")
SWAP = [(i, i ^ 1) for i in range(2 * SIDE * SIDE)]


def mm(a, b, dims):
    return lax.dot_general(a, b, dims, preferred_element_type=jnp.float32)


def stacked(ref, i):
    rows = pl.ds(i * BLK, BLK)
    return jnp.concatenate([ref[rows, :HD], ref[rows, HD:]], axis=0)


def unstack(ref, i, value):
    rows = pl.ds(i * BLK, BLK)
    ref[rows, :HD] = value[:BLK]
    ref[rows, HD:] = value[BLK:]


def load(kv, meta, plane, ch, cols):
    return jnp.concatenate([kv[pl.ds(row_of(meta, plane, ch, j), BLK), cols] for j in range(CHUNK)], axis=0)


def row_of(meta, plane, ch, j):
    return pl.multiple_of(meta[ROWS_AT + plane * LIST + ch * CHUNK + j] * BLK, BLK)


def scores_of(keys, q, meta, vec, plane, ch, i):
    s = mm(keys, q, NT)
    sub = lax.broadcasted_iota(jnp.int32, (BLK, LANES), 0)
    qstart, qpos = vec[pl.ds(2 * i, 1), :], vec[pl.ds(2 * i + 1, 1), :]
    parts = []
    for j in range(CHUNK):
        first = meta[plane * LIST + ch * CHUNK + j] * BLK
        ok = (sub >= qstart - first) & (sub <= qpos - first)
        parts.append(jnp.where(ok, s[j * BLK : (j + 1) * BLK], NEG))
    return jnp.concatenate(parts, axis=0)


def each_chunk(meta, plane, body):
    split, total = meta[COUNT_AT + 2 * plane], meta[COUNT_AT + 2 * plane + 1]

    def run(first, count):
        for ch in range(count):
            body(first + ch, jnp.where(first + ch >= split, 1, 0))

    def trip(t, _):
        run(4 * t, 4)
        return 0

    lax.fori_loop(0, total >> 2, trip, 0)
    rest = total & ~3
    for count in range(1, 4):
        pl.when((total & 3) == count)(lambda count=count: run(rest, count))


def chunk_at(ch):
    return pl.ds(pl.multiple_of(ch * CHUNK * BLK, CHUNK * BLK), CHUNK * BLK)


def forward(meta, vec, plane, kv, q_st, top, total, out, s_ref, p_ref, old_top=None):
    def scores(ch, i):
        s = scores_of(load(kv, meta, plane, ch, KEYS), q_st[i], meta, vec, plane, ch, i)
        s_ref[chunk_at(ch), :] = s
        row = pl.ds(i, 1)
        top[row, :] = jnp.maximum(top[row, :], jnp.max(s, axis=0, keepdims=True))

    each_chunk(meta, plane, scores)
    if old_top is not None:
        for i in range(2):
            row = slice(i, i + 1)
            shrink = jnp.exp2((old_top[i] - top[row, :]) * SCALE2)
            total[row, :] = total[row, :] * shrink
            out[i] = out[i] * shrink

    def outputs(ch, i):
        row = pl.ds(i, 1)
        p = jnp.exp2((s_ref[chunk_at(ch), :] - top[row, :]) * SCALE2)
        total[row, :] = total[row, :] + jnp.sum(p, axis=0, keepdims=True)
        p = p.astype(jnp.bfloat16)
        if p_ref is not None:
            p_ref[chunk_at(ch), :] = p
        out[i] = out[i] + mm(load(kv, meta, plane, ch, VALS), p, TN)

    each_chunk(meta, plane, outputs)


def first_pass(order, lengths, q_ref, kv, meta, vec, stat, part, q_st, s_ref, top, total, table):
    me = lax.axis_index("ctx")
    core = me & 1
    for s in range(NBLK):
        dev = s // 2
        y, x, c = dev // (2 * SIDE), (dev // 2) % SIDE, dev % 2
        slot = (y * SIDE + x if c else x * SIDE + y) * 2 + s % 2
        table[order[s]] = slot + (HALF * (1 - core) if c else HALF * core)
    lane = lax.broadcasted_iota(jnp.int32, (1, LANES), 1) & (BLK - 1)
    mine, others = jnp.int32(0), jnp.int32(LIST)
    for i in range(2):
        blk = order[2 * me + i]
        qpos = blk * BLK + lane
        end, low = jnp.int32(0), jnp.int32(0)
        qstart = jnp.zeros((1, LANES), jnp.int32)
        for d in range(NDOC):
            end = end + lengths[d]
            qstart = jnp.where(qpos >= end, end, qstart)
            low = jnp.where(blk * BLK >= end, end, low)
        vec[2 * i : 2 * i + 1, :] = qstart
        vec[2 * i + 1 : 2 * i + 2, :] = qpos
        low = low >> 7
        for j in range(REACH):
            p = blk - j
            slot = table[jnp.maximum(p, 0)]
            away = slot >= HALF
            at = jnp.where(away, others, mine)
            meta[at] = p
            meta[ROWS_AT + at] = slot & (HALF - 1)
            step = jnp.where(p >= low, 1, 0)
            others = others + jnp.where(away, step, 0)
            mine = mine + jnp.where(away, 0, step)
        for j in range(CHUNK - 1):
            for at in (mine, others):
                meta[at + j] = -1024
                meta[ROWS_AT + at + j] = 0
        mine = (mine + CHUNK - 1) // CHUNK * CHUNK
        others = (others + CHUNK - 1) // CHUNK * CHUNK
        meta[COUNT_AT + i] = mine // CHUNK
        meta[COUNT_AT + 2 + i] = (others - LIST) // CHUNK
        q_st[i] = stacked(q_ref, i)
    top[...] = jnp.full_like(top, NEG)
    total[...] = jnp.zeros_like(total)
    part[...] = jnp.zeros_like(part)
    forward(meta, vec, 0, kv, q_st, top, total, part, s_ref, None)
    stat[pl.ds(0, 2), :] = top[...]
    stat[pl.ds(2, 2), :] = total[...]


def put(ref, meta, plane, ch, dk, dv):
    for j in range(CHUNK):
        to = pl.ds(row_of(meta, plane, ch, j), BLK)
        rows = slice(j * BLK, (j + 1) * BLK)
        ref[to, KEYS] = (ref[to, KEYS].astype(jnp.float32) + dk[rows]).astype(jnp.bfloat16)
        ref[to, VALS] = (ref[to, VALS].astype(jnp.float32) + dv[rows]).astype(jnp.bfloat16)


def second_pass(
    meta, vec, stat, q_ref, g_ref, part, kv, o_ref, lse, dq_ref, dkv,
    q_st, g_st, over, s_ref, p_ref, top, total, out, scaled
):
    dkv[...] = jnp.zeros_like(dkv)
    dq_ref[...] = jnp.zeros_like(dq_ref)
    for i in range(2):
        q_st[i], g_st[i] = stacked(q_ref, i), stacked(g_ref, i)
    top[...] = stat[pl.ds(0, 2), :]
    total[...] = stat[pl.ds(2, 2), :]
    out[...] = part[...]
    forward(meta, vec, 1, kv, q_st, top, total, out, s_ref, p_ref, [stat[i : i + 1, :] for i in range(2)])
    for i in range(2):
        row = slice(i, i + 1)
        inv = 1.0 / total[row, :]
        att = (out[i] * inv).T.astype(jnp.bfloat16)
        unstack(o_ref, i, att)
        wide = g_st[i].astype(jnp.float32)
        lse[i : i + 1, :] = top[row, :] * SCALE2 + jnp.log2(total[row, :])
        lse[2 + i : 3 + i, :] = jnp.sum((wide * att.astype(jnp.float32)).T, axis=0, keepdims=True)
        scaled[row, :] = inv * SCALE
        over[i] = (wide * jnp.broadcast_to(inv, (HD, LANES)).T).astype(jnp.bfloat16)

    def grads(ch, i):
        p = p_ref[chunk_at(ch), :]
        dp = mm(load(kv, meta, 1, ch, VALS), g_st[i], NT)
        ds = ((p.astype(jnp.float32) * scaled[pl.ds(i, 1), :]) * (dp - lse[pl.ds(2 + i, 1), :])).astype(jnp.bfloat16)
        put(dkv, meta, 1, ch, mm(ds, q_st[i], NN), mm(p, over[i], NN))
        dq_ref[i] = dq_ref[i] + mm(load(kv, meta, 1, ch, KEYS), ds, TN)

    each_chunk(meta, 1, grads)


def third_pass(meta, vec, lse, q_ref, g_ref, dq_in, att_in, kv, o_ref, dq_ref, dkv, q_st, g_st, dq):
    o_ref[...] = att_in[...]
    dkv[...] = jnp.zeros_like(dkv)
    dq[...] = dq_in[...]
    for i in range(2):
        q_st[i], g_st[i] = stacked(q_ref, i), stacked(g_ref, i)

    def grads(ch, i):
        keys = load(kv, meta, 0, ch, KEYS)
        s = scores_of(keys, q_st[i], meta, vec, 0, ch, i)
        p = jnp.exp2(s * SCALE2 - lse[pl.ds(i, 1), :])
        dp = mm(load(kv, meta, 0, ch, VALS), g_st[i], NT)
        ds = ((p * SCALE) * (dp - lse[pl.ds(2 + i, 1), :])).astype(jnp.bfloat16)
        put(dkv, meta, 0, ch, mm(ds, q_st[i], NN), mm(p.astype(jnp.bfloat16), g_st[i], NN))
        dq[i] = dq[i] + mm(keys, ds, TN)

    each_chunk(meta, 0, grads)
    for i in range(2):
        unstack(dq_ref, i, dq[i].T.astype(jnp.bfloat16))


SMEM = pl.BlockSpec(memory_space=pltpu.SMEM)
VMEM = pl.BlockSpec(memory_space=pltpu.VMEM)


def shape(*dims, dtype=jnp.bfloat16):
    return jax.ShapeDtypeStruct(dims, dtype)


def kernel(body, name, ins, outs, out_specs, scratch, flops, size):
    return pl.pallas_call(
        body,
        out_shape=outs,
        in_specs=ins,
        out_specs=out_specs,
        scratch_shapes=scratch,
        compiler_params=pltpu.CompilerParams(vmem_limit_bytes=24 * 1024 * 1024),
        cost_estimate=pl.CostEstimate(flops=flops, bytes_accessed=size, transcendentals=0),
        name=name,
    )


def per_device(queries, key_rows, value_rows, grad_output, doc_lengths, block_order):
    tokens = queries.shape[0]
    f32, i32, bf16 = jnp.float32, jnp.int32, jnp.bfloat16
    plane = HALF * BLK
    scores = pltpu.VMEM((LIST * BLK, LANES), f32)
    weights = pltpu.VMEM((LIST * BLK, LANES), bf16)
    rows = pltpu.VMEM((2, LANES, HD), bf16)
    pair = pltpu.VMEM((2, LANES), f32)
    sums = pltpu.VMEM((2, HD, LANES), f32)
    kv = jnp.concatenate([key_rows, value_rows], axis=1)
    kv = (kv.astype(f32) * LIFT).astype(jnp.float16)
    line = jnp.broadcast_to(kv[None], (SIDE, tokens, 2 * HD))
    line = lax.all_to_all(line, "ctx", 0, 0, tiled=True, axis_index_groups=FIRST)
    line = line.reshape(SIDE * tokens, 2 * HD)
    own = lax.all_gather(line, "ctx", axis=0, tiled=True, axis_index_groups=SECOND)
    own = (own.astype(f32) * (1 / LIFT)).astype(bf16)
    oth = lax.ppermute(own, "ctx", SWAP)
    wide = shape(2, HD, LANES, dtype=f32)
    small = shape(4, LANES, dtype=f32)
    meta, vec, stat, part = kernel(
        first_pass,
        "forward_own",
        [SMEM, SMEM, VMEM, VMEM],
        (shape(META, dtype=i32), shape(4, LANES, dtype=i32), small, wide),
        (SMEM, VMEM, VMEM, VMEM),
        [rows, scores, pair, pair, pltpu.SMEM((NBLK,), i32)],
        2 * 10**9,
        4 * 10**6,
    )(block_order, doc_lengths, queries, own)
    att, lse, dq, dkv_oth = kernel(
        second_pass,
        "other_plane",
        [SMEM, VMEM, VMEM, VMEM, VMEM, VMEM, VMEM],
        (shape(tokens, 2 * HD), small, wide, shape(plane, 2 * HD)),
        (VMEM,) * 4,
        [rows, rows, rows, scores, weights, pair, pair, sums, pair],
        4 * 10**9,
        6 * 10**6,
    )(meta, vec, stat, queries, grad_output, part, oth)
    back = lax.ppermute(dkv_oth, "ctx", SWAP)
    attention, grad_queries, dkv_own = kernel(
        third_pass,
        "backward_own",
        [SMEM, VMEM, VMEM, VMEM, VMEM, VMEM, VMEM, VMEM],
        (shape(tokens, 2 * HD), shape(tokens, 2 * HD), shape(plane, 2 * HD)),
        (VMEM,) * 3,
        [rows, rows, sums],
        3 * 10**9,
        6 * 10**6,
    )(meta, vec, lse, queries, grad_output, dq, att, own)
    part = (dkv_own.astype(f32) + back.astype(f32)).astype(bf16)
    part = part.reshape(SIDE, SIDE * tokens, 2 * HD)
    part = lax.all_to_all(part, "ctx", 0, 0, tiled=True, axis_index_groups=SECOND)
    part = jnp.sum(part.astype(f32), axis=0).astype(bf16).reshape(SIDE, tokens, 2 * HD)
    part = lax.all_to_all(part, "ctx", 0, 0, tiled=True, axis_index_groups=FIRST)
    part = jnp.sum(part.astype(f32), axis=0).astype(bf16)
    return attention, grad_queries, part[:, :HD], part[:, HD:]


def solution(mesh):
    rows = P(("dp", "ctx"), None)
    return jax.shard_map(
        per_device,
        mesh=mesh,
        in_specs=(rows, rows, rows, rows, P("dp"), P("dp")),
        out_specs=(rows, rows, rows, rows),
        check_vma=False,
    )
```
